256 devices in a mesh: dp: 4 (over y), seq: 64 (over z, x, core).
Axes of the slice: x: 4, y: 4, z: 8, core: 2. Of those that a mesh axis runs over, the one named last changes fastest.
Arguments:
- query_tokens: bfloat16 [131072, 1024], P(('dp', 'seq')), parts along dimension 0, may hold values from -6 to 6
- key_tokens: bfloat16 [131072, 1024], P(('dp', 'seq')), parts along dimension 0, may hold values from -6 to 6
- value_tokens: bfloat16 [131072, 1024], P(('dp', 'seq')), parts along dimension 0, may hold values from -6 to 6
- gate_tokens: bfloat16 [131072, 1024], P(('dp', 'seq')), parts along dimension 0, may hold values from -6 to 6
- filter_taps: float32 [27, 1024], replicated, may hold values from -1.25 to 1.25
- selected: int32 [2048, 8, 8], P(('dp', 'seq')), parts along dimension 0, may hold values from 0 to 511, as said below
- cotangent: bfloat16 [131072, 1024], P(('dp', 'seq')), parts along dimension 0, may hold values from -6 to 6
Outputs:
- attended: bfloat16 [131072, 1024], P(('dp', 'seq')), parts along dimension 0
- query_gradient: bfloat16 [131072, 1024], P(('dp', 'seq')), parts along dimension 0
- key_gradient: bfloat16 [131072, 1024], P(('dp', 'seq')), parts along dimension 0
- value_gradient: bfloat16 [131072, 1024], P(('dp', 'seq')), parts along dimension 0
- gate_gradient: bfloat16 [131072, 1024], P(('dp', 'seq')), parts along dimension 0
- filter_gradient: float32 [108, 1024], P('dp'), parts along dimension 0
The draws below stay inside these ranges and needn't reach their ends.
There are 4 independent parts, one for each index of `dp`. The reference program is written for one: setup_inputs(seed, part) draws one part's arguments, and reference() takes and returns one part's arrays. A program takes and returns all parts, laid end to end along the dimension named above; an argument that names none is the same for every part. Nothing has to cross between parts.
Inputs may be any that keep to these rules, and one draw needn't show every extreme that they name: `selected`: for each query cube and head the 8 entries are distinct. Over the 8 query cubes of one device, the pairs of key cube and head that lie on other devices number exactly 96, at most 3 of them on any one other device; in every draw one device receives exactly 3 such pairs from every other device.
All inputs are finite; a program needn't handle non-finite values.
Results may differ from the reference program's by a relative error of at most 0.0075.
The reference program's roundings to bfloat16 on the way count: a program that leaves them out, or rounds other values in their place, can miss the bound.
Values may be sent and summed in bfloat16 or wider, within the bound.
No kernel may reach another device: no remote copies, remote signals or barrier semaphores. Data moves between devices by JAX's collectives and lax.ppermute only.
A program may use at most 192 MiB of HBM per device.

```python
import jax
import jax.numpy as jnp
from jax import lax

HEAD_DIM = 128
HEADS = 8
WIDTH = 1024
SLABS = 4
TOPK = 8
POOL = 12
FRAME_ROWS = 8
CUBES_DEV = 8
NCUBES = 512
TOKENS = 32768
CAP = 3


def selection(key):
    device_count = NCUBES // CUBES_DEV
    pair_count = CUBES_DEV * HEADS
    remote = HEADS * POOL
    slot_count = (device_count - 1) * CAP
    busiest = jax.random.randint(jax.random.fold_in(key, 1), (), 0, device_count)

    def one_source(source):
        source_key = jax.random.fold_in(jax.random.fold_in(key, 2), source)
        target = jnp.where(source == busiest, (busiest + 1) % device_count, busiest)
        target_offset = (target - source - 1) % device_count
        ranking = jax.random.permutation(jax.random.fold_in(source_key, 3), slot_count)
        slot_owner = jnp.arange(slot_count) // CAP
        ranking = jnp.where(slot_owner == target_offset, ranking + slot_count, ranking)
        _, chosen = lax.top_k(ranking, remote)
        owner_device = (source + 1 + chosen // CAP) % device_count
        offset = jax.random.randint(jax.random.fold_in(source_key, 4), (device_count,), 0, pair_count)
        pair_index = (chosen % CAP + offset[owner_device]) % pair_count
        far_cube = owner_device * CUBES_DEV + pair_index // HEADS
        far_head = pair_index % HEADS
        same_head = far_head[:, None] == far_head[None, :]
        earlier = jnp.arange(remote)[None, :] < jnp.arange(remote)[:, None]
        head_rank = jnp.sum((same_head & earlier).astype(jnp.int32), axis=1)
        head_ids = jnp.arange(HEADS)
        cube_ids = jnp.arange(CUBES_DEV)
        candidates = CUBES_DEV + remote
        noise_bits = jax.random.randint(jax.random.fold_in(source_key, 5), (CUBES_DEV, HEADS, candidates), 0, 65536)
        logit_matrix = noise_bits * candidates + jnp.arange(candidates)
        eligible = far_head[None, None, :] == head_ids[None, :, None]
        forced = eligible & (head_rank[None, None, :] % CUBES_DEV == cube_ids[:, None, None])
        far_score = jnp.where(forced, logit_matrix[:, :, CUBES_DEV:] + (1 << 26), jnp.where(eligible, logit_matrix[:, :, CUBES_DEV:], -1))
        logit_matrix = jnp.concatenate([logit_matrix[:, :, :CUBES_DEV], far_score], axis=2)
        _, picked = lax.top_k(logit_matrix, TOPK)
        lookup = jnp.concatenate([source * CUBES_DEV + cube_ids, far_cube])
        return lookup[picked]
    picks = jax.vmap(one_source)(jnp.arange(device_count))
    return picks.reshape(NCUBES, HEADS, TOPK).astype(jnp.int32)


def cube_field(key, common_scale, token_scale):
    channels = HEADS * HEAD_DIM
    common = jax.random.normal(jax.random.fold_in(key, 1), (NCUBES, 1, channels), jnp.float32)
    single = jax.random.normal(jax.random.fold_in(key, 2), (NCUBES, 64, channels), jnp.float32)
    sampled = common_scale * common + token_scale * single
    return jnp.clip(sampled, -6.0, 6.0).reshape(TOKENS, channels)


def draw_query_tokens(key, part):
    sampled = cube_field(jax.random.fold_in(key, 31), 1.3, 0.8)
    return sampled.astype(jnp.bfloat16)


def draw_key_tokens(key, part):
    sampled = cube_field(jax.random.fold_in(key, 32), 1.3, 0.8)
    return sampled.astype(jnp.bfloat16)


def draw_value_tokens(key, part):
    return cube_field(jax.random.fold_in(key, 33), 1.0, 0.8).astype(jnp.bfloat16)


def draw_selected(key, part):
    return selection(key)


def level_of(key, dims, shards, low, high):
    loudness = 1.0
    for dim, shards_of in shards:
        draws = jax.random.uniform(jax.random.fold_in(jax.random.fold_in(key, 6), dim), (shards_of,), jnp.float32, low / len(shards), high / len(shards))
        loudness = loudness * jnp.repeat(jnp.exp(draws), dims[dim] // shards_of).reshape((-1,) + (1,) * (len(dims) - 1 - dim))
    return loudness


def gaussian(stream_key, extent, width, reach, pieces=(), kind=jnp.bfloat16):
    result = width * jax.random.normal(stream_key, extent, jnp.float32)
    if pieces:
        result = result * level_of(stream_key, extent, pieces, -0.22, 0.18)
    return jnp.clip(result, -reach, reach).astype(kind)


def setup_inputs(seed: int = 0, part: int = 0) -> dict:
    key_of = jax.random.split(jax.random.key(seed), 8)
    part_keys = jax.random.split(jax.random.fold_in(key_of[7], part), 8)
    query_tokens = draw_query_tokens(jax.random.fold_in(jax.random.fold_in(key_of[7], part), 71), part)
    key_tokens = draw_key_tokens(jax.random.fold_in(jax.random.fold_in(key_of[7], part), 71), part)
    value_tokens = draw_value_tokens(jax.random.fold_in(jax.random.fold_in(key_of[7], part), 71), part)
    gate_tokens = gaussian(part_keys[3], (TOKENS, WIDTH), 1.0, 6.0, ((0, 64),))
    filter_taps = gaussian(key_of[4], (27, WIDTH), 27 ** -0.5, 1.25, (), jnp.float32)
    selected = draw_selected(jax.random.fold_in(jax.random.fold_in(key_of[7], part), 71), part)
    cotangent = gaussian(part_keys[6], (TOKENS, WIDTH), 1.0, 6.0, ((0, 64),))
    return dict(query_tokens=query_tokens, key_tokens=key_tokens, value_tokens=value_tokens, gate_tokens=gate_tokens, filter_taps=filter_taps, selected=selected, cotangent=cotangent)


def upcast_precision(rounded_result):
    return lax.optimization_barrier(rounded_result).astype(jnp.float32)


def to_blocks(tokens):
    cube_count = tokens.shape[0] // 64
    return tokens.reshape(cube_count, 64, HEADS, HEAD_DIM).transpose(0, 2, 1, 3)


def from_blocks(blocks):
    cube_count = blocks.shape[0]
    return blocks.transpose(0, 2, 1, 3).reshape(cube_count * 64, HEADS * HEAD_DIM)


def to_lattice(tokens):
    channels = tokens.shape[1]
    block_count = 2 * SLABS * FRAME_ROWS
    blocks = tokens.reshape(block_count, CUBES_DEV * 64, channels)
    rotated = jnp.roll(blocks, 2 * FRAME_ROWS + FRAME_ROWS // 2, axis=0)
    lattice = rotated.reshape(2, SLABS, FRAME_ROWS, CUBES_DEV, 4, 4, 4, channels).transpose(1, 4, 2, 5, 0, 3, 6, 7)
    return lattice.reshape(SLABS * 4, FRAME_ROWS * 4, 2 * CUBES_DEV * 4, channels)


def from_lattice(lattice):
    channels = lattice.shape[3]
    block_count = 2 * SLABS * FRAME_ROWS
    rotated = lattice.reshape(SLABS, 4, FRAME_ROWS, 4, 2, CUBES_DEV, 4, channels).transpose(4, 0, 2, 5, 1, 3, 6, 7)
    rotated = rotated.reshape(block_count, CUBES_DEV * 64, channels)
    blocks = jnp.roll(rotated, -(2 * FRAME_ROWS + FRAME_ROWS // 2), axis=0)
    return blocks.reshape(block_count * CUBES_DEV * 64, channels)


def convolve_values(framed, filter_taps):
    frames = framed.shape[0] - 2
    height = framed.shape[1]
    breadth = framed.shape[2]
    padded = jnp.pad(framed, ((0, 0), (1, 1), (1, 1), (0, 0)))
    totaled_sum = jnp.zeros((frames, height, breadth, framed.shape[3]), jnp.float32)
    for back_step in range(3):
        for row_step in (-1, 0, 1):
            for col_step in (-1, 0, 1):
                tap_index = back_step * 9 + (row_step + 1) * 3 + col_step + 1
                shifted = padded[2 - back_step:2 - back_step + frames, 1 + row_step:1 + row_step + height, 1 + col_step:1 + col_step + breadth]
                totaled_sum = totaled_sum + filter_taps[tap_index] * shifted.astype(jnp.float32)
    return totaled_sum


def convolve_back(padded_grad, framed, filter_taps):
    frames = padded_grad.shape[0] - 2
    height = padded_grad.shape[1]
    breadth = padded_grad.shape[2]
    grad_space = jnp.pad(padded_grad, ((0, 0), (1, 1), (1, 1), (0, 0)))
    value_space = jnp.pad(framed, ((0, 0), (1, 1), (1, 1), (0, 0)))
    inner_grad = padded_grad[:frames]
    totaled_sum = jnp.zeros(inner_grad.shape, jnp.float32)
    tap_rows = []
    for back_step in range(3):
        for row_step in (-1, 0, 1):
            for col_step in (-1, 0, 1):
                tap_index = back_step * 9 + (row_step + 1) * 3 + col_step + 1
                totaled_sum = totaled_sum + filter_taps[tap_index] * grad_space[back_step:back_step + frames, 1 - row_step:1 - row_step + height, 1 - col_step:1 - col_step + breadth]
                shifted = value_space[2 - back_step:2 - back_step + frames, 1 + row_step:1 + row_step + height, 1 + col_step:1 + col_step + breadth]
                tap_rows.append(jnp.sum(inner_grad * shifted.astype(jnp.float32), axis=(0, 1, 2)))
    return totaled_sum, jnp.stack(tap_rows)


def pool_cubes(tokens):
    return jnp.mean(tokens.astype(jnp.float32).reshape(tokens.shape[0] // 64, 64, tokens.shape[1]), axis=1)


def separate_heads(rows):
    return rows.reshape(rows.shape[0], HEADS, HEAD_DIM)


def coarse_forward(averaged_query, averaged_key, averaged_value, logit_scale):
    logit_matrix = jnp.einsum("agt,ogt->gao", upcast_precision(separate_heads(averaged_query)), upcast_precision(separate_heads(averaged_key))) * logit_scale
    row_max = jnp.max(logit_matrix, axis=2, keepdims=True)
    exponent = jnp.exp(logit_matrix - row_max)
    weights = exponent / jnp.sum(exponent, axis=2, keepdims=True)
    rounded_result = weights.astype(jnp.bfloat16)
    blended_output = jnp.einsum("clx,xcu->lcu", upcast_precision(rounded_result), upcast_precision(separate_heads(averaged_value)))
    return weights, rounded_result, blended_output.reshape(blended_output.shape[0], HEADS * HEAD_DIM)


def coarse_delta(averaged_gradient, coarse_out):
    return jnp.sum(upcast_precision(separate_heads(averaged_gradient)) * separate_heads(coarse_out), axis=2).T


def score_grads(weights, averaged_gradient, averaged_value, row_delta):
    weight_gradient_total = jnp.einsum("agt,ogt->gao", upcast_precision(separate_heads(averaged_gradient)), upcast_precision(separate_heads(averaged_value)))
    return (weights * (weight_gradient_total - row_delta[:, :, None])).astype(jnp.bfloat16)


def query_side(logit_gradient, averaged_key, logit_scale):
    totaled_sum = jnp.einsum("clx,xcu->lcu", upcast_precision(logit_gradient), upcast_precision(separate_heads(averaged_key))) * logit_scale
    return totaled_sum.reshape(totaled_sum.shape[0], HEADS * HEAD_DIM)


def key_side(logit_gradient, rounded_result, averaged_query, averaged_gradient, logit_scale):
    key_portion = jnp.einsum("opk,poe->koe", upcast_precision(logit_gradient), upcast_precision(separate_heads(averaged_query))) * logit_scale
    value_portion = jnp.einsum("opk,poe->koe", upcast_precision(rounded_result), upcast_precision(separate_heads(averaged_gradient)))
    key_count = key_portion.shape[0]
    return jnp.concatenate([key_portion.reshape(key_count, -1), value_portion.reshape(key_count, -1)], axis=1)


def attend_cube(table_key, table_value, query_cube, grad_cube, row_cube, logit_scale):
    head_count, pick_count = row_cube.shape
    flat_rows = row_cube.reshape(-1)
    key_rows = table_key[flat_rows].reshape(head_count, pick_count * 64, HEAD_DIM).astype(jnp.float32)
    value_rows = table_value[flat_rows].reshape(head_count, pick_count * 64, HEAD_DIM).astype(jnp.float32)
    query_wide = query_cube.astype(jnp.float32)
    grad_wide = grad_cube.astype(jnp.float32)
    logit_matrix = jnp.einsum("hqd,hkd->hqk", query_wide, key_rows) * logit_scale
    row_max = jnp.max(logit_matrix, axis=2, keepdims=True)
    exponent = jnp.exp(logit_matrix - row_max)
    weights = exponent / jnp.sum(exponent, axis=2, keepdims=True)
    rounded_result = upcast_precision(weights.astype(jnp.bfloat16))
    fine_out = jnp.einsum("hqk,hkd->hqd", rounded_result, value_rows)
    row_delta = jnp.sum(grad_wide * fine_out, axis=2, keepdims=True)
    weight_gradient_total = jnp.einsum("hqd,hkd->hqk", grad_wide, value_rows)
    logit_gradient = upcast_precision((weights * (weight_gradient_total - row_delta)).astype(jnp.bfloat16))
    query_grad = jnp.einsum("hqk,hkd->hqd", logit_gradient, key_rows) * logit_scale
    key_grad = jnp.einsum("hqk,hqd->hkd", logit_gradient, query_wide) * logit_scale
    value_grad = jnp.einsum("hqk,hqd->hkd", rounded_result, grad_wide)
    return fine_out, query_grad, key_grad.reshape(head_count * pick_count, 64, HEAD_DIM), value_grad.reshape(head_count * pick_count, 64, HEAD_DIM)


def fine_pass(query_tokens, key_tokens, filtered, cotangent, selected, logit_scale):
    table_key = to_blocks(key_tokens).reshape(-1, 64, HEAD_DIM)
    table_value = to_blocks(filtered).reshape(-1, 64, HEAD_DIM)
    table_row = (selected * HEADS + jnp.arange(HEADS, dtype=jnp.int32)[None, :, None]).astype(jnp.int32)

    def scan_step(accumulated, inputs):
        key_acc, value_acc = accumulated
        query_cube, grad_cube, row_cube = inputs
        fine_out, query_grad, key_grad, value_grad = attend_cube(table_key, table_value, query_cube, grad_cube, row_cube, logit_scale)
        flat_rows = row_cube.reshape(-1)
        return (key_acc.at[flat_rows].add(key_grad), value_acc.at[flat_rows].add(value_grad)), (fine_out, query_grad)

    zeros_table = jnp.zeros((table_key.shape[0], 64, HEAD_DIM), jnp.float32)
    (key_acc, value_acc), (fine_out, fine_query) = lax.scan(scan_step, (zeros_table, zeros_table), (to_blocks(query_tokens), to_blocks(cotangent), table_row))
    cube_count = fine_out.shape[0]
    fine_key = from_blocks(key_acc.reshape(cube_count, HEADS, 64, HEAD_DIM))
    fine_value = from_blocks(value_acc.reshape(cube_count, HEADS, 64, HEAD_DIM))
    return from_blocks(fine_out), from_blocks(fine_query), fine_key, fine_value


def reference(query_tokens, key_tokens, value_tokens, gate_tokens, filter_taps, selected, cotangent):
    logit_scale = HEAD_DIM ** -0.5
    channels = HEADS * HEAD_DIM
    lattice = to_lattice(value_tokens)
    framed = jnp.concatenate([jnp.zeros((2,) + lattice.shape[1:], lattice.dtype), lattice], axis=0)
    filtered = from_lattice(convolve_values(framed, filter_taps)).astype(jnp.bfloat16)
    averaged_query = pool_cubes(query_tokens).astype(jnp.bfloat16)
    averaged_key = pool_cubes(key_tokens).astype(jnp.bfloat16)
    averaged_value = pool_cubes(filtered).astype(jnp.bfloat16)
    gated = cotangent.astype(jnp.float32) * gate_tokens.astype(jnp.float32)
    averaged_gradient = jnp.sum(gated.reshape(-1, 64, channels), axis=1).astype(jnp.bfloat16)
    weights, rounded_result, coarse_out = coarse_forward(averaged_query, averaged_key, averaged_value, logit_scale)
    row_delta = coarse_delta(averaged_gradient, coarse_out)
    logit_gradient = score_grads(weights, averaged_gradient, averaged_value, row_delta)
    coarse_query = query_side(logit_gradient, averaged_key, logit_scale)
    shares = key_side(logit_gradient, rounded_result, averaged_query, averaged_gradient, logit_scale)
    fine_tokens, fine_query, fine_key, fine_value = fine_pass(query_tokens, key_tokens, filtered, cotangent, selected, logit_scale)
    coarse_tokens = jnp.repeat(coarse_out, 64, axis=0)
    attended = (fine_tokens + gate_tokens.astype(jnp.float32) * coarse_tokens).astype(jnp.bfloat16)
    gate_gradient = (cotangent.astype(jnp.float32) * coarse_tokens).astype(jnp.bfloat16)
    query_gradient = (fine_query + jnp.repeat(coarse_query, 64, axis=0) / 64.0).astype(jnp.bfloat16)
    key_gradient = (fine_key + jnp.repeat(shares[:, :channels], 64, axis=0) / 64.0).astype(jnp.bfloat16)
    filtered_grad = fine_value + jnp.repeat(shares[:, channels:], 64, axis=0) / 64.0
    grad_lattice = to_lattice(filtered_grad)
    padded_grad = jnp.concatenate([grad_lattice, jnp.zeros((2,) + grad_lattice.shape[1:], jnp.float32)], axis=0)
    value_lattice, tap_grads = convolve_back(padded_grad, framed, filter_taps)
    value_gradient = from_lattice(value_lattice).astype(jnp.bfloat16)
    return attended, query_gradient, key_gradient, value_gradient, gate_gradient, tap_grads
```

```python
import functools
import jax
import jax.numpy as jnp
from jax import lax
from jax.experimental import pallas as pl
from jax.experimental.pallas import tpu as pltpu
from jax.sharding import PartitionSpec as P

HEAD_DIM = 128
HEADS = 8
SLABS = 4
POOL = 12
BF = jnp.bfloat16
F32 = jnp.float32
TRAILER = 8
VMEM = pltpu.CompilerParams(vmem_limit_bytes=56 << 20)


def head_lanes(h):
    if isinstance(h, int):
        return slice(h * HEAD_DIM, (h + 1) * HEAD_DIM)
    return pl.ds(pl.multiple_of(h * HEAD_DIM, HEAD_DIM), HEAD_DIM)


def cube_rows(c):
    if isinstance(c, int):
        return slice(c * 64, c * 64 + 64)
    return pl.ds(pl.multiple_of(c * 64, 64), 64)


def mm(a, b, dims):
    return lax.dot_general(a, b, (dims, ((), ())), preferred_element_type=F32)


def whole(shape):
    zeros = (0,) * len(shape)
    return pl.BlockSpec(shape, lambda *_: zeros)


def gather_body(pairs, tokens, *rest, dests, slots):
    extra, out = rest if len(rest) == 2 else (None, rest[0])
    base = pl.program_id(0) * dests

    def one(d, carry):
        for s in range(slots):
            p = pairs[(base + d) * slots + s]
            out[d, cube_rows(s)] = tokens[cube_rows(p // HEADS), head_lanes(p % HEADS)]
        if extra is not None:
            out[d, slots * 64 :] = extra[d % HEADS]
        return carry

    lax.fori_loop(0, dests, one, 0, unroll=2)


def gather_pairs(pairs, tokens, devices, extra=None):
    slots = pairs.shape[0] // devices
    dests = devices // 4
    rows = slots * 64 + (0 if extra is None else extra.shape[1])
    operands = (tokens,) if extra is None else (tokens, extra)
    return pl.pallas_call(
        functools.partial(gather_body, dests=dests, slots=slots),
        grid_spec=pltpu.PrefetchScalarGridSpec(
            num_scalar_prefetch=1,
            grid=(4,),
            in_specs=[whole(x.shape) for x in operands],
            out_specs=pl.BlockSpec((dests, rows, HEAD_DIM), lambda i, *_: (i, 0, 0)),
        ),
        out_shape=jax.ShapeDtypeStruct((devices, rows, HEAD_DIM), tokens.dtype),
        compiler_params=VMEM,
        name="gather_pairs",
    )(pairs, *operands)


def fill_table(table, tokens, fetched, pairs, slots):
    for p in range(pairs):
        table[p] = tokens[cube_rows(p // HEADS), head_lanes(p % HEADS)]

    def one(d, carry):
        for s in range(slots):
            table[pairs + d * slots + s] = fetched[d, cube_rows(s)]
        return carry

    lax.fori_loop(0, fetched.shape[0], one, 0, unroll=2)


def clear(acc):
    def one(i, carry):
        acc[i] = jnp.zeros(acc.shape[1:], acc.dtype)
        return carry

    lax.fori_loop(0, acc.shape[0], one, 0, unroll=4)


def flush(acc, own, far, pairs, slots):
    def near(i, carry):
        own[i] = acc[i]
        return carry

    def distant(d, carry):
        for s in range(slots):
            far[d, cube_rows(s)] = acc[pairs + d * slots + s].astype(far.dtype)
        far[d, slots * 64 :] = jnp.zeros((far.shape[1] - slots * 64, HEAD_DIM), far.dtype)
        return carry

    lax.fori_loop(0, pairs, near, 0, unroll=4)
    lax.fori_loop(0, far.shape[0], distant, 0, unroll=2)


def picked(rows, cube, h):
    return [rows[(cube * HEADS + h) * 8 + i] for i in range(8)]


def probs_body(rows, query, grad, keys, far_keys, weights, own, far, table, acc, *, scale, pairs, slots):
    cube = pl.program_id(0)

    @pl.when(cube == 0)
    def _():
        fill_table(table, keys, far_keys, pairs, slots)
        clear(acc)

    def one_head(h):
        lanes = head_lanes(h)
        rs = picked(rows, cube, h)
        key_rows = jnp.concatenate([table[r] for r in rs], axis=0)
        logits = mm(query[:, lanes], key_rows, ((1,), (1,))) * scale
        expo = jnp.exp(logits - jnp.max(logits, axis=1, keepdims=True))
        w = expo / jnp.sum(expo, axis=1, keepdims=True)
        weights[h] = w
        part = mm(w.astype(BF), grad[:, lanes], ((0,), (0,)))
        for i, r in enumerate(rs):
            acc[r] += part[64 * i : 64 * i + 64]

    for h in range(HEADS):
        one_head(h)

    @pl.when(cube == pl.num_programs(0) - 1)
    def _():
        flush(acc, own, far, pairs, slots)


def fine_probs(rows, query, grad, keys, far_keys, slots, scale):
    cubes = query.shape[0] // 64
    pairs = cubes * HEADS
    devices = far_keys.shape[0]
    far_shape = (devices, slots * 64 + TRAILER, HEAD_DIM)
    width = HEADS * HEAD_DIM
    cube_block = pl.BlockSpec((64, width), lambda c, *_: (c, 0))
    return pl.pallas_call(
        functools.partial(probs_body, scale=scale, pairs=pairs, slots=slots),
        grid_spec=pltpu.PrefetchScalarGridSpec(
            num_scalar_prefetch=1,
            grid=(cubes,),
            in_specs=[cube_block, cube_block, whole(keys.shape), whole(far_keys.shape)],
            out_specs=[
                pl.BlockSpec((HEADS, 64, 512), lambda c, *_: (c, 0, 0)),
                whole((pairs, 64, HEAD_DIM)),
                whole(far_shape),
            ],
            scratch_shapes=[
                pltpu.VMEM((pairs + devices * slots, 64, HEAD_DIM), BF),
                pltpu.VMEM((pairs + devices * slots, 64, HEAD_DIM), F32),
            ],
        ),
        out_shape=[
            jax.ShapeDtypeStruct((pairs, 64, 512), F32),
            jax.ShapeDtypeStruct((pairs, 64, HEAD_DIM), F32),
            jax.ShapeDtypeStruct(far_shape, BF),
        ],
        compiler_params=VMEM,
        name="fine_probs",
    )(rows, query, grad, keys, far_keys)


def grads_body(
    rows, query, grad, keys, far_keys, values, far_values, weights,
    fine_out, fine_query, own, far, key_table, value_table, acc, *, scale, pairs, slots,
):
    cube = pl.program_id(0)

    @pl.when(cube == 0)
    def _():
        fill_table(key_table, keys, far_keys, pairs, slots)
        fill_table(value_table, values, far_values, pairs, slots)
        clear(acc)

    def one_head(h):
        lanes = head_lanes(h)
        rs = picked(rows, cube, h)
        key_rows = jnp.concatenate([key_table[r] for r in rs], axis=0)
        value_rows = jnp.concatenate([value_table[r] for r in rs], axis=0)
        g = grad[:, lanes]
        w = weights[h]
        out = mm(w.astype(BF), value_rows, ((1,), (0,)))
        delta = jnp.sum(g.astype(F32) * out, axis=1, keepdims=True)
        slope = mm(g, value_rows, ((1,), (1,)))
        ds = (w * (slope - delta)).astype(BF)
        fine_out[:, lanes] = out
        fine_query[:, lanes] = mm(ds, key_rows, ((1,), (0,))) * scale
        part = mm(ds, query[:, lanes], ((0,), (0,))) * scale
        for i, r in enumerate(rs):
            acc[r] += part[64 * i : 64 * i + 64]

    for h in range(HEADS):
        one_head(h)

    @pl.when(cube == pl.num_programs(0) - 1)
    def _():
        flush(acc, own, far, pairs, slots)


def fine_grads(rows, query, grad, keys, far_keys, values, far_values, weights, slots, scale):
    cubes = query.shape[0] // 64
    pairs = cubes * HEADS
    devices = far_keys.shape[0]
    far_shape = (devices, slots * 64 + TRAILER, HEAD_DIM)
    width = HEADS * HEAD_DIM
    cube_block = pl.BlockSpec((64, width), lambda c, *_: (c, 0))
    table = (pairs + devices * slots, 64, HEAD_DIM)
    return pl.pallas_call(
        functools.partial(grads_body, scale=scale, pairs=pairs, slots=slots),
        grid_spec=pltpu.PrefetchScalarGridSpec(
            num_scalar_prefetch=1,
            grid=(cubes,),
            in_specs=[
                cube_block,
                cube_block,
                whole(keys.shape),
                whole(far_keys.shape),
                whole(values.shape),
                whole(far_values.shape),
                pl.BlockSpec((HEADS, 64, 512), lambda c, *_: (c, 0, 0)),
            ],
            out_specs=[
                cube_block,
                cube_block,
                whole((pairs, 64, HEAD_DIM)),
                whole(far_shape),
            ],
            scratch_shapes=[
                pltpu.VMEM(table, BF),
                pltpu.VMEM(table, BF),
                pltpu.VMEM(table, F32),
            ],
        ),
        out_shape=[
            jax.ShapeDtypeStruct(query.shape, F32),
            jax.ShapeDtypeStruct(query.shape, F32),
            jax.ShapeDtypeStruct((pairs, 64, HEAD_DIM), F32),
            jax.ShapeDtypeStruct(far_shape, BF),
        ],
        compiler_params=VMEM,
        name="fine_grads",
    )(rows, query, grad, keys, far_keys, values, far_values, weights)


def collect_body(pairs, own, back, share, out, acc):
    for p in range(own.shape[0]):
        c, h = p // HEADS, p % HEADS
        acc[cube_rows(c), head_lanes(h)] = own[p] + share[c : c + 1, head_lanes(h)] * (1.0 / 64.0)

    slots = pairs.shape[0] // back.shape[0]

    def one(d, carry):
        for s in range(slots):
            p = pairs[d * slots + s]
            rows = cube_rows(p // HEADS)
            lanes = head_lanes(p % HEADS)
            acc[rows, lanes] += back[d, cube_rows(s)].astype(F32)
        return carry

    lax.fori_loop(0, back.shape[0], one, 0)
    out[...] = acc[...].astype(out.dtype)


def collect(pairs, own, back, share, dtype):
    shape = (own.shape[0] // HEADS * 64, HEADS * HEAD_DIM)
    return pl.pallas_call(
        collect_body,
        grid_spec=pltpu.PrefetchScalarGridSpec(
            num_scalar_prefetch=1,
            grid=(1,),
            in_specs=[whole(own.shape), whole(back.shape), whole(share.shape)],
            out_specs=whole(shape),
            scratch_shapes=[pltpu.VMEM(shape, F32)],
        ),
        out_shape=jax.ShapeDtypeStruct(shape, dtype),
        compiler_params=VMEM,
        name="collect",
    )(pairs, own, back, share)


def put_halves(target, sem, stage, parts):
    for i, part in enumerate(parts):
        high = part.astype(BF)
        stage[:, i] = high
        stage[:, len(parts) + i] = (part - high.astype(F32)).astype(BF)
    rows = target.shape[1]
    copy = pltpu.make_async_copy(
        stage, target.at[:, pl.ds(rows - TRAILER, TRAILER)], sem
    )
    copy.start()
    copy.wait()


def from_halves(received):
    halves = received[:, -TRAILER:].astype(F32)
    return halves[:, : TRAILER // 2] + halves[:, TRAILER // 2 :]


def coarse_body(block, query, key, grad, value, back, out, stage, sem, *, scale):
    del back
    q, k, g, v = query[...], key[...], grad[...], value[...]
    logits = mm(k, q, ((1,), (1,))) * scale
    expo = jnp.exp(logits - jnp.max(logits, axis=0, keepdims=True))
    w = expo / jnp.sum(expo, axis=0, keepdims=True)
    wr = w.astype(BF)
    slope = mm(v, g, ((1,), (1,)))
    delta = jnp.sum(wr.astype(F32) * slope, axis=0, keepdims=True)
    ds = (w * (slope - delta)).astype(BF)
    results = (
        mm(wr, v, ((0,), (0,))),
        mm(ds, k, ((0,), (0,))) * scale,
        mm(ds, q, ((1,), (0,))) * scale,
        mm(wr, g, ((1,), (0,))),
    )
    shape = (results[0].shape[0] // 8, 8, HEAD_DIM)
    mine = lax.broadcasted_iota(jnp.int32, shape, 1) == block[0]
    parts = [jnp.sum(jnp.where(mine, r.reshape(shape), 0.0), axis=1) for r in results]
    put_halves(out, sem, stage, parts)


def coarse_head(block, pooled, back, scale):
    anywhere = pl.BlockSpec(memory_space=pl.ANY)
    return pl.pallas_call(
        functools.partial(coarse_body, scale=scale),
        grid_spec=pltpu.PrefetchScalarGridSpec(
            num_scalar_prefetch=1,
            grid=(1,),
            in_specs=[whole(x.shape) for x in pooled] + [anywhere],
            out_specs=anywhere,
            scratch_shapes=[
                pltpu.VMEM((back.shape[0], TRAILER, HEAD_DIM), BF),
                pltpu.SemaphoreType.DMA,
            ],
        ),
        out_shape=jax.ShapeDtypeStruct(back.shape, back.dtype),
        input_output_aliases={5: 0},
        compiler_params=VMEM,
        name="coarse_head",
    )(block, *pooled, back)


def taps_body(grad, framed, out, wide):
    frames, height, breadth = grad.shape[:3]
    planes, rows = framed.shape[:2]
    for t in range(planes):
        for r in range(rows):
            wide[t * rows + r, 0 : framed.shape[2]] = framed[t, r].astype(F32)
    for col in range(3):
        sums = {}
        for t in range(planes):
            for r in range(rows):
                cells = wide[t * rows + r, col : col + breadth]
                for back in range(3):
                    for row in range(3):
                        f, y = t - 2 + back, r - row
                        if 0 <= f < frames and 0 <= y < height:
                            tap = 9 * back + 3 * row + col
                            term = jnp.sum((grad[f, y] * cells).reshape(-1, 8, 128), axis=0)
                            sums[tap] = sums[tap] + term if tap in sums else term
        for tap, total in sums.items():
            out[tap : tap + 1] = jnp.sum(total, axis=0, keepdims=True)
    out[27:] = jnp.zeros((out.shape[0] - 27, 128), F32)


def tap_gradients(grad, framed):
    width = grad.shape[3]
    return pl.pallas_call(
        taps_body,
        grid=(width // 128,),
        in_specs=[
            pl.BlockSpec(grad.shape[:3] + (128,), lambda i: (0, 0, 0, i)),
            pl.BlockSpec(framed.shape[:3] + (128,), lambda i: (0, 0, 0, i)),
        ],
        out_specs=pl.BlockSpec((32, 128), lambda i: (0, i)),
        scratch_shapes=[pltpu.VMEM((framed.shape[0] * framed.shape[1], 40, 128), F32)],
        out_shape=jax.ShapeDtypeStruct((32, width), F32),
        compiler_params=VMEM,
        name="tap_gradients",
    )(grad, framed)


def sum_body(shares, back, out, stage, sem):
    del back
    total = shares[0]
    for d in range(1, shares.shape[0]):
        total = total + shares[d]
    for i in range(TRAILER // 2):
        high = total[i : i + 1].astype(BF)
        low = (total[i : i + 1] - high.astype(F32)).astype(BF)
        for half, row in ((0, high), (TRAILER // 2, low)):
            stage[:, half + i] = jnp.broadcast_to(row, (stage.shape[0], HEAD_DIM))
    copy = pltpu.make_async_copy(
        stage, out.at[:, pl.ds(out.shape[1] - TRAILER, TRAILER)], sem
    )
    copy.start()
    copy.wait()


def sum_taps(shares, back):
    anywhere = pl.BlockSpec(memory_space=pl.ANY)
    return pl.pallas_call(
        sum_body,
        in_specs=[pl.BlockSpec(memory_space=pltpu.VMEM), anywhere],
        out_specs=anywhere,
        scratch_shapes=[
            pltpu.VMEM((back.shape[0], TRAILER, HEAD_DIM), BF),
            pltpu.SemaphoreType.DMA,
        ],
        out_shape=jax.ShapeDtypeStruct(back.shape, back.dtype),
        input_output_aliases={1: 0},
        compiler_params=VMEM,
        name="sum_taps",
    )(shares, back)


def from_partner(block, axis, apart):
    count = lax.axis_size(axis)
    route = []
    for low in range(count):
        high = low | 1 << apart
        if high != low and high < count:
            route += [(low, high), (high, low)]
    return lax.ppermute(block, axis, route)


def with_halo(cells, sides, width):
    for axis, dim in sides:
        count = lax.axis_size(axis)
        head = lax.slice_in_dim(cells, 0, width, axis=dim)
        tail = lax.slice_in_dim(cells, cells.shape[dim] - width, cells.shape[dim], axis=dim)
        cells = jnp.concatenate(
            [
                lax.ppermute(tail, axis, [(i, (i + 1) % count) for i in range(count)]),
                cells,
                lax.ppermute(head, axis, [((i + 1) % count, i) for i in range(count)]),
            ],
            axis=dim,
        )
    return cells


def passed_along(value, axis, steps):
    count = lax.axis_size(axis)
    pairs = [(source, (source + steps) % count) for source in range(count)]
    return lax.ppermute(value, axis, pairs)


def to_lattice(tokens):
    channels = tokens.shape[1]
    cube_count = tokens.shape[0] // 64
    lattice = tokens.reshape(cube_count, 4, 4, 4, channels).transpose(1, 2, 0, 3, 4)
    return lattice.reshape(4, 4, cube_count * 4, channels)


def from_lattice(lattice):
    channels = lattice.shape[3]
    cube_count = lattice.shape[2] // 4
    tokens = lattice.reshape(4, 4, cube_count, 4, channels).transpose(2, 0, 1, 3, 4)
    return tokens.reshape(cube_count * 64, channels)


def side_columns(lattice, edge, col_half):
    blank = jnp.zeros_like(edge)
    return jnp.concatenate(
        [jnp.where(col_half == 1, edge, blank), lattice, jnp.where(col_half == 0, edge, blank)],
        axis=2,
    )


def clear_rims(extended, row_band, band_count):
    blank = jnp.zeros_like(extended[:, :1])
    upper = jnp.where(row_band > 0, extended[:, :1], blank)
    lower = jnp.where(row_band < band_count - 1, extended[:, -1:], blank)
    return jnp.concatenate([upper, extended[:, 1:-1], lower], axis=1)


def convolve_values(framed, filter_taps):
    frames = framed.shape[0] - 2
    height = framed.shape[1] - 2
    breadth = framed.shape[2] - 2
    totaled_sum = jnp.zeros((frames, height, breadth, framed.shape[3]), jnp.float32)
    for back_step in range(3):
        for row_step in (-1, 0, 1):
            for col_step in (-1, 0, 1):
                tap_index = back_step * 9 + (row_step + 1) * 3 + col_step + 1
                shifted = framed[
                    2 - back_step : 2 - back_step + frames,
                    1 + row_step : 1 + row_step + height,
                    1 + col_step : 1 + col_step + breadth,
                ]
                totaled_sum = totaled_sum + filter_taps[tap_index] * shifted.astype(jnp.float32)
    return totaled_sum


def convolve_back(grad_space, filter_taps):
    frames = grad_space.shape[0] - 2
    height = grad_space.shape[1] - 2
    breadth = grad_space.shape[2] - 2
    total = jnp.zeros((frames, height, breadth, grad_space.shape[3]), F32)
    for back_step in range(3):
        for row_step in (-1, 0, 1):
            for col_step in (-1, 0, 1):
                tap_index = back_step * 9 + (row_step + 1) * 3 + col_step + 1
                total = total + filter_taps[tap_index] * grad_space[
                    back_step : back_step + frames,
                    1 - row_step : 1 - row_step + height,
                    1 - col_step : 1 - col_step + breadth,
                ]
    return total


def pool_cubes(tokens):
    return jnp.mean(
        tokens.astype(jnp.float32).reshape(tokens.shape[0] // 64, 64, tokens.shape[1]), axis=1
    )


def spread(per_cube):
    cube_count = per_cube.shape[0]
    return jnp.broadcast_to(per_cube[:, None, :], (cube_count, 64, per_cube.shape[1])).reshape(
        cube_count * 64, per_cube.shape[1]
    )


def exchanged(rows):
    return lax.all_to_all(rows, "seq", split_axis=0, concat_axis=0, tiled=True)


def after(value, *earlier):
    return lax.optimization_barrier((value, *earlier))[0]


def shards(query_tokens, key_tokens, value_tokens, gate_tokens, filter_taps, selected, cotangent):
    devices = lax.axis_size("seq")
    device_index = lax.axis_index("seq")
    cube_count = query_tokens.shape[0] // 64
    pair_count = cube_count * HEADS
    channels = HEADS * HEAD_DIM
    capacity = max(3, 2 * HEADS * POOL // (devices - 1))
    logit_scale = HEAD_DIM ** (-0.5)
    band_count = devices // (2 * SLABS)
    rotated = (device_index + 2 * band_count + band_count // 2) % devices
    row_band = rotated % band_count
    slab_index = rotated // band_count % SLABS
    col_half = rotated // (devices // 2)
    col_bit = devices.bit_length() - 2

    owner_device = selected // cube_count
    pair_index = selected % cube_count * HEADS + jnp.arange(HEADS, dtype=jnp.int32)[None, :, None]
    remote_flat = (owner_device != device_index).reshape(-1)
    pair_codes = (owner_device * pair_count + pair_index).reshape(-1)
    matches = (
        pair_codes[:, None] == jnp.arange(devices * pair_count, dtype=jnp.int32)[None, :]
    ) & remote_flat[:, None]
    present = jnp.any(matches, axis=0).reshape(devices, pair_count).astype(jnp.int32)
    slot_rank = jnp.cumsum(present, axis=1) - present
    in_slot = (slot_rank[:, :, None] == jnp.arange(capacity, dtype=jnp.int32)[None, None, :]) & (
        present[:, :, None] > 0
    )
    requests = jnp.sum(
        in_slot.astype(jnp.int32) * jnp.arange(pair_count, dtype=jnp.int32)[None, :, None], axis=1
    ).reshape(-1)
    asked_pairs = exchanged(requests)
    slot_of = jnp.sum(matches.astype(jnp.int32) * slot_rank.reshape(-1)[None, :], axis=1)
    table_row = jnp.where(
        remote_flat,
        pair_count + owner_device.reshape(-1) * capacity + slot_of,
        pair_index.reshape(-1),
    )

    lattice = to_lattice(value_tokens)
    value_edge = from_partner(
        jnp.where(col_half == 0, lattice[:, :, -1:], lattice[:, :, :1]), "seq", col_bit
    )
    value_wide = side_columns(lattice, value_edge, col_half)
    value_tall = clear_rims(with_halo(value_wide, (("seq", 1),), 1), row_band, band_count)
    prior_frames = passed_along(value_tall[-2:], "seq", band_count)
    prior_frames = jnp.where(slab_index > 0, prior_frames, jnp.zeros_like(prior_frames))
    framed = jnp.concatenate([prior_frames, value_tall], axis=0)

    far_keys = exchanged(after(gather_pairs(asked_pairs, key_tokens, devices), framed))

    filtered = from_lattice(convolve_values(framed, filter_taps)).astype(BF)
    gated = cotangent.astype(F32) * gate_tokens.astype(F32)
    pooled = jnp.stack(
        [
            pool_cubes(query_tokens).astype(BF),
            pool_cubes(key_tokens).astype(BF),
            jnp.sum(gated.reshape(cube_count, 64, channels), axis=1).astype(BF),
            pool_cubes(filtered).astype(BF),
        ],
        axis=1,
    )
    pooled = pooled.reshape(cube_count, 4, HEADS, HEAD_DIM).transpose(2, 1, 0, 3)
    pooled = pooled.reshape(HEADS, 4 * cube_count, HEAD_DIM)
    far_values = exchanged(after(gather_pairs(asked_pairs, filtered, devices, pooled), far_keys))
    one_head = far_values[:, capacity * 64 :].reshape(devices, 4, cube_count, HEAD_DIM)
    one_head = one_head.transpose(1, 0, 2, 3).reshape(4, devices * cube_count, HEAD_DIM)

    weights, own_value, back_value = fine_probs(
        table_row, query_tokens, cotangent, key_tokens, far_keys, capacity, logit_scale
    )
    block = (device_index // HEADS).reshape(1)
    back_value = exchanged(coarse_head(block, tuple(one_head), back_value, logit_scale))
    fine_out, fine_query, own_key, back_key = fine_grads(
        table_row, query_tokens, cotangent, key_tokens, far_keys, filtered, far_values, weights,
        capacity, logit_scale,
    )
    coarse = from_halves(back_value).reshape(cube_count, HEADS, 4, HEAD_DIM)
    coarse = coarse.transpose(2, 0, 1, 3).reshape(4, cube_count, channels)
    coarse_out, coarse_query, coarse_key, coarse_value = coarse

    coarse_tokens = spread(coarse_out)
    attended = (fine_out + gate_tokens.astype(F32) * coarse_tokens).astype(BF)
    gate_gradient = (cotangent.astype(F32) * coarse_tokens).astype(BF)
    query_gradient = (fine_query + spread(coarse_query) / 64.0).astype(BF)

    filtered_grad = collect(
        asked_pairs, after(own_value, back_key), back_value, coarse_value, F32
    )
    grad_lattice = to_lattice(filtered_grad)
    grad_edge = from_partner(
        jnp.where(col_half == 0, grad_lattice[:, :, -1:], grad_lattice[:, :, :1]).astype(BF),
        "seq",
        col_bit,
    ).astype(F32)
    grad_wide = side_columns(grad_lattice, grad_edge, col_half)
    grad_tall = clear_rims(with_halo(grad_wide, (("seq", 1),), 1), row_band, band_count)
    next_frames = passed_along(grad_tall[:2].astype(BF), "seq", -band_count).astype(F32)
    next_frames = jnp.where(slab_index < SLABS - 1, next_frames, jnp.zeros_like(next_frames))
    grad_space = jnp.concatenate([grad_tall, next_frames], axis=0)
    shares = exchanged(tap_gradients(grad_lattice, framed).reshape(devices, TRAILER // 2, HEAD_DIM))
    back_key = exchanged(after(sum_taps(shares, back_key), grad_space))
    filter_gradient = from_halves(back_key).reshape(-1, channels)[: filter_taps.shape[0]]
    value_gradient = from_lattice(convolve_back(grad_space, filter_taps)).astype(BF)
    key_gradient = collect(asked_pairs, own_key, back_key, coarse_key, BF)
    return (attended, query_gradient, key_gradient, value_gradient, gate_gradient, filter_gradient)


def solution(mesh):
    return jax.shard_map(
        shards,
        mesh=mesh,
        in_specs=(
            P(("dp", "seq"), None),
            P(("dp", "seq"), None),
            P(("dp", "seq"), None),
            P(("dp", "seq"), None),
            P(),
            P(("dp", "seq"), None, None),
            P(("dp", "seq"), None),
        ),
        out_specs=(
            P(("dp", "seq"), None),
            P(("dp", "seq"), None),
            P(("dp", "seq"), None),
            P(("dp", "seq"), None),
            P(("dp", "seq"), None),
            P("dp", None),
        ),
        check_vma=False,
    )
```

```python
import functools
import jax
import jax.numpy as jnp
from jax import lax
from jax.experimental import pallas as pl
from jax.experimental.pallas import tpu as pltpu
from jax.sharding import PartitionSpec as P

HEAD_DIM = 128
HEADS = 8
SLABS = 4
POOL = 12
BF = jnp.bfloat16
F32 = jnp.float32
TRAILER = 8
VMEM = pltpu.CompilerParams(vmem_limit_bytes=56 << 20)


def head_lanes(h):
    if isinstance(h, int):
        return slice(h * HEAD_DIM, (h + 1) * HEAD_DIM)
    return pl.ds(pl.multiple_of(h * HEAD_DIM, HEAD_DIM), HEAD_DIM)


def cube_rows(c):
    if isinstance(c, int):
        return slice(c * 64, c * 64 + 64)
    return pl.ds(pl.multiple_of(c * 64, 64), 64)


def mm(a, b, dims):
    return lax.dot_general(a, b, (dims, ((), ())), preferred_element_type=F32)


def whole(shape):
    zeros = (0,) * len(shape)
    return pl.BlockSpec(shape, lambda *_: zeros)


def gather_body(pairs, tokens, *rest, dests, slots):
    extra, out = rest if len(rest) == 2 else (None, rest[0])
    base = pl.program_id(0) * dests

    def one(d, carry):
        for s in range(slots):
            p = pairs[(base + d) * slots + s]
            out[d, cube_rows(s)] = tokens[cube_rows(p // HEADS), head_lanes(p % HEADS)]
        if extra is not None:
            out[d, slots * 64 :] = extra[d % HEADS]
        return carry

    lax.fori_loop(0, dests, one, 0, unroll=2)


def gather_pairs(pairs, tokens, devices, extra=None):
    slots = pairs.shape[0] // devices
    dests = devices // 4
    rows = slots * 64 + (0 if extra is None else extra.shape[1])
    operands = (tokens,) if extra is None else (tokens, extra)
    return pl.pallas_call(
        functools.partial(gather_body, dests=dests, slots=slots),
        grid_spec=pltpu.PrefetchScalarGridSpec(
            num_scalar_prefetch=1,
            grid=(4,),
            in_specs=[whole(x.shape) for x in operands],
            out_specs=pl.BlockSpec((dests, rows, HEAD_DIM), lambda i, *_: (i, 0, 0)),
        ),
        out_shape=jax.ShapeDtypeStruct((devices, rows, HEAD_DIM), tokens.dtype),
        compiler_params=VMEM,
        name="gather_pairs",
    )(pairs, *operands)


def fill_table(table, tokens, fetched, pairs, slots):
    for p in range(pairs):
        table[p] = tokens[cube_rows(p // HEADS), head_lanes(p % HEADS)]

    def one(d, carry):
        for s in range(slots):
            table[pairs + d * slots + s] = fetched[d, cube_rows(s)]
        return carry

    lax.fori_loop(0, fetched.shape[0], one, 0, unroll=2)


def clear(acc):
    def one(i, carry):
        acc[i] = jnp.zeros(acc.shape[1:], acc.dtype)
        return carry

    lax.fori_loop(0, acc.shape[0], one, 0, unroll=4)


def flush(acc, own, far, pairs, slots):
    def near(i, carry):
        own[i] = acc[i]
        return carry

    def distant(d, carry):
        for s in range(slots):
            far[d, cube_rows(s)] = acc[pairs + d * slots + s].astype(far.dtype)
        far[d, slots * 64 :] = jnp.zeros((far.shape[1] - slots * 64, HEAD_DIM), far.dtype)
        return carry

    lax.fori_loop(0, pairs, near, 0, unroll=4)
    lax.fori_loop(0, far.shape[0], distant, 0, unroll=2)


def picked(rows, cube, h):
    return [rows[(cube * HEADS + h) * 8 + i] for i in range(8)]


def probs_body(rows, query, grad, keys, far_keys, weights, own, far, table, acc, *, scale, pairs, slots):
    cube = pl.program_id(0)

    @pl.when(cube == 0)
    def _():
        fill_table(table, keys, far_keys, pairs, slots)
        clear(acc)

    def one_head(h):
        lanes = head_lanes(h)
        rs = picked(rows, cube, h)
        key_rows = jnp.concatenate([table[r] for r in rs], axis=0)
        logits = mm(query[:, lanes], key_rows, ((1,), (1,))) * scale
        expo = jnp.exp(logits - jnp.max(logits, axis=1, keepdims=True))
        w = expo / jnp.sum(expo, axis=1, keepdims=True)
        weights[h] = w
        part = mm(w.astype(BF), grad[:, lanes], ((0,), (0,)))
        for i, r in enumerate(rs):
            acc[r] += part[64 * i : 64 * i + 64]

    def two_heads(i, carry):
        one_head(2 * i)
        one_head(2 * i + 1)
        return carry

    lax.fori_loop(0, HEADS // 2, two_heads, 0)

    @pl.when(cube == pl.num_programs(0) - 1)
    def _():
        flush(acc, own, far, pairs, slots)


def fine_probs(rows, query, grad, keys, far_keys, slots, scale):
    cubes = query.shape[0] // 64
    pairs = cubes * HEADS
    devices = far_keys.shape[0]
    far_shape = (devices, slots * 64 + TRAILER, HEAD_DIM)
    width = HEADS * HEAD_DIM
    cube_block = pl.BlockSpec((64, width), lambda c, *_: (c, 0))
    return pl.pallas_call(
        functools.partial(probs_body, scale=scale, pairs=pairs, slots=slots),
        grid_spec=pltpu.PrefetchScalarGridSpec(
            num_scalar_prefetch=1,
            grid=(cubes,),
            in_specs=[cube_block, cube_block, whole(keys.shape), whole(far_keys.shape)],
            out_specs=[
                pl.BlockSpec((HEADS, 64, 512), lambda c, *_: (c, 0, 0)),
                whole((pairs, 64, HEAD_DIM)),
                whole(far_shape),
            ],
            scratch_shapes=[
                pltpu.VMEM((pairs + devices * slots, 64, HEAD_DIM), BF),
                pltpu.VMEM((pairs + devices * slots, 64, HEAD_DIM), F32),
            ],
        ),
        out_shape=[
            jax.ShapeDtypeStruct((pairs, 64, 512), F32),
            jax.ShapeDtypeStruct((pairs, 64, HEAD_DIM), F32),
            jax.ShapeDtypeStruct(far_shape, BF),
        ],
        compiler_params=VMEM,
        name="fine_probs",
    )(rows, query, grad, keys, far_keys)


def grads_body(
    rows, query, grad, keys, far_keys, values, far_values, weights,
    fine_out, fine_query, own, far, key_table, value_table, acc, *, scale, pairs, slots,
):
    cube = pl.program_id(0)

    @pl.when(cube == 0)
    def _():
        fill_table(key_table, keys, far_keys, pairs, slots)
        fill_table(value_table, values, far_values, pairs, slots)
        clear(acc)

    def one_head(h):
        lanes = head_lanes(h)
        rs = picked(rows, cube, h)
        key_rows = jnp.concatenate([key_table[r] for r in rs], axis=0)
        value_rows = jnp.concatenate([value_table[r] for r in rs], axis=0)
        g = grad[:, lanes]
        w = weights[h]
        out = mm(w.astype(BF), value_rows, ((1,), (0,)))
        delta = jnp.sum(g.astype(F32) * out, axis=1, keepdims=True)
        slope = mm(g, value_rows, ((1,), (1,)))
        ds = (w * (slope - delta)).astype(BF)
        fine_out[:, lanes] = out
        fine_query[:, lanes] = mm(ds, key_rows, ((1,), (0,))) * scale
        part = mm(ds, query[:, lanes], ((0,), (0,))) * scale
        for i, r in enumerate(rs):
            acc[r] += part[64 * i : 64 * i + 64]

    def two_heads(i, carry):
        one_head(2 * i)
        one_head(2 * i + 1)
        return carry

    lax.fori_loop(0, HEADS // 2, two_heads, 0)

    @pl.when(cube == pl.num_programs(0) - 1)
    def _():
        flush(acc, own, far, pairs, slots)


def fine_grads(rows, query, grad, keys, far_keys, values, far_values, weights, slots, scale):
    cubes = query.shape[0] // 64
    pairs = cubes * HEADS
    devices = far_keys.shape[0]
    far_shape = (devices, slots * 64 + TRAILER, HEAD_DIM)
    width = HEADS * HEAD_DIM
    cube_block = pl.BlockSpec((64, width), lambda c, *_: (c, 0))
    table = (pairs + devices * slots, 64, HEAD_DIM)
    return pl.pallas_call(
        functools.partial(grads_body, scale=scale, pairs=pairs, slots=slots),
        grid_spec=pltpu.PrefetchScalarGridSpec(
            num_scalar_prefetch=1,
            grid=(cubes,),
            in_specs=[
                cube_block,
                cube_block,
                whole(keys.shape),
                whole(far_keys.shape),
                whole(values.shape),
                whole(far_values.shape),
                pl.BlockSpec((HEADS, 64, 512), lambda c, *_: (c, 0, 0)),
            ],
            out_specs=[
                cube_block,
                cube_block,
                whole((pairs, 64, HEAD_DIM)),
                whole(far_shape),
            ],
            scratch_shapes=[
                pltpu.VMEM(table, BF),
                pltpu.VMEM(table, BF),
                pltpu.VMEM(table, F32),
            ],
        ),
        out_shape=[
            jax.ShapeDtypeStruct(query.shape, F32),
            jax.ShapeDtypeStruct(query.shape, F32),
            jax.ShapeDtypeStruct((pairs, 64, HEAD_DIM), F32),
            jax.ShapeDtypeStruct(far_shape, BF),
        ],
        compiler_params=VMEM,
        name="fine_grads",
    )(rows, query, grad, keys, far_keys, values, far_values, weights)


def collect_body(pairs, own, back, trailer, out, acc, *, quantity):
    slots = pairs.shape[0] // back.shape[0]
    for p in range(own.shape[0]):
        c, h = p // HEADS, p % HEADS
        high = trailer[p, quantity : quantity + 1].astype(F32)
        low = trailer[p, TRAILER // 2 + quantity : TRAILER // 2 + quantity + 1].astype(F32)
        acc[cube_rows(c), head_lanes(h)] = own[p] + (high + low) * (1.0 / 64.0)

    def one(d, carry):
        for s in range(slots):
            p = pairs[d * slots + s]
            rows = cube_rows(p // HEADS)
            lanes = head_lanes(p % HEADS)
            acc[rows, lanes] += back[d, cube_rows(s)].astype(F32)
        return carry

    lax.fori_loop(0, back.shape[0], one, 0)
    if len(out.shape) == 2:
        out[...] = acc[...].astype(out.dtype)
        return

    def lane_block(h, carry):
        lanes = head_lanes(h)
        for g in range(acc.shape[0] // 64):
            for i in range(16):
                row = 64 * g + 4 * i
                out[i // 4, i % 4, 4 * g : 4 * g + 4, lanes] = acc[row : row + 4, lanes]
        return carry

    lax.fori_loop(0, HEADS, lane_block, 0)


def collect(pairs, own, back, halves, quantity, lattice):
    cubes = own.shape[0] // HEADS
    width = HEADS * HEAD_DIM
    tokens = (cubes * 64, width)
    shape, dtype = ((4, 4, 4 * cubes, width), F32) if lattice else (tokens, BF)
    last = halves.shape[1] // TRAILER - 1
    return pl.pallas_call(
        functools.partial(collect_body, quantity=quantity),
        grid_spec=pltpu.PrefetchScalarGridSpec(
            num_scalar_prefetch=1,
            grid=(1,),
            in_specs=[
                whole(own.shape),
                whole(back.shape),
                pl.BlockSpec((halves.shape[0], TRAILER, HEAD_DIM), lambda *_: (0, last, 0)),
            ],
            out_specs=whole(shape),
            scratch_shapes=[pltpu.VMEM(tokens, F32)],
        ),
        out_shape=jax.ShapeDtypeStruct(shape, dtype),
        compiler_params=VMEM,
        name="collect",
    )(pairs, own, back, halves)


def put_halves(target, sem, stage, parts):
    for i, part in enumerate(parts):
        high = part.astype(BF)
        stage[:, i] = high
        stage[:, len(parts) + i] = (part - high.astype(F32)).astype(BF)
    rows = target.shape[1]
    copy = pltpu.make_async_copy(
        stage, target.at[:, pl.ds(rows - TRAILER, TRAILER)], sem
    )
    copy.start()
    copy.wait()


def from_halves(received):
    halves = received[:, -TRAILER:].astype(F32)
    return halves[:, : TRAILER // 2] + halves[:, TRAILER // 2 :]


def coarse_body(block, query, key, grad, value, back, out, stage, sem, *, scale):
    del back
    q, k, g, v = query[...], key[...], grad[...], value[...]
    logits = mm(k, q, ((1,), (1,))) * scale
    expo = jnp.exp(logits - jnp.max(logits, axis=0, keepdims=True))
    w = expo / jnp.sum(expo, axis=0, keepdims=True)
    wr = w.astype(BF)
    slope = mm(v, g, ((1,), (1,)))
    delta = jnp.sum(wr.astype(F32) * slope, axis=0, keepdims=True)
    ds = (w * (slope - delta)).astype(BF)
    results = (
        mm(wr, v, ((0,), (0,))),
        mm(ds, k, ((0,), (0,))) * scale,
        mm(ds, q, ((1,), (0,))) * scale,
        mm(wr, g, ((1,), (0,))),
    )
    shape = (results[0].shape[0] // 8, 8, HEAD_DIM)
    mine = lax.broadcasted_iota(jnp.int32, shape, 1) == block[0]
    parts = [jnp.sum(jnp.where(mine, r.reshape(shape), 0.0), axis=1) for r in results]
    put_halves(out, sem, stage, parts)


def coarse_head(block, pooled, back, scale):
    anywhere = pl.BlockSpec(memory_space=pl.ANY)
    return pl.pallas_call(
        functools.partial(coarse_body, scale=scale),
        grid_spec=pltpu.PrefetchScalarGridSpec(
            num_scalar_prefetch=1,
            grid=(1,),
            in_specs=[whole(x.shape) for x in pooled] + [anywhere],
            out_specs=anywhere,
            scratch_shapes=[
                pltpu.VMEM((back.shape[0], TRAILER, HEAD_DIM), BF),
                pltpu.SemaphoreType.DMA,
            ],
        ),
        out_shape=jax.ShapeDtypeStruct(back.shape, back.dtype),
        input_output_aliases={5: 0},
        compiler_params=VMEM,
        name="coarse_head",
    )(block, *pooled, back)


def taps_body(grad, framed, out, wide):
    frames, height, breadth = grad.shape[:3]
    planes, rows = framed.shape[:2]
    for t in range(planes):
        for r in range(rows):
            wide[t * rows + r, 0 : framed.shape[2]] = framed[t, r].astype(F32)
    for col in range(3):
        sums = {}
        for t in range(planes):
            for r in range(rows):
                cells = wide[t * rows + r, col : col + breadth]
                for back in range(3):
                    for row in range(3):
                        f, y = t - 2 + back, r - row
                        if 0 <= f < frames and 0 <= y < height:
                            tap = 9 * back + 3 * row + col
                            term = jnp.sum((grad[f, y] * cells).reshape(-1, 8, 128), axis=0)
                            sums[tap] = sums[tap] + term if tap in sums else term
        for tap, total in sums.items():
            out[tap // 4, 0, tap % 4 : tap % 4 + 1] = jnp.sum(total, axis=0, keepdims=True)
    out[6, 0, 3:] = jnp.zeros((1, 128), F32)
    out[7, 0] = jnp.zeros((4, 128), F32)


def tap_gradients(grad, framed):
    width = grad.shape[3]
    return pl.pallas_call(
        taps_body,
        grid=(width // 128,),
        in_specs=[
            pl.BlockSpec(grad.shape[:3] + (128,), lambda i: (0, 0, 0, i)),
            pl.BlockSpec(framed.shape[:3] + (128,), lambda i: (0, 0, 0, i)),
        ],
        out_specs=pl.BlockSpec((8, 1, 4, 128), lambda i: (0, i, 0, 0)),
        scratch_shapes=[pltpu.VMEM((framed.shape[0] * framed.shape[1], 40, 128), F32)],
        out_shape=jax.ShapeDtypeStruct((8, width // 128, 4, 128), F32),
        compiler_params=VMEM,
        name="tap_gradients",
    )(grad, framed)


def sum_body(shares, back, out, stage, sem):
    del back
    total = shares[0]
    for d in range(1, shares.shape[0]):
        total = total + shares[d]
    for i in range(TRAILER // 2):
        high = total[i : i + 1].astype(BF)
        low = (total[i : i + 1] - high.astype(F32)).astype(BF)
        for half, row in ((0, high), (TRAILER // 2, low)):
            stage[:, half + i] = jnp.broadcast_to(row, (stage.shape[0], HEAD_DIM))
    copy = pltpu.make_async_copy(
        stage, out.at[:, pl.ds(out.shape[1] - TRAILER, TRAILER)], sem
    )
    copy.start()
    copy.wait()


def sum_taps(shares, back):
    anywhere = pl.BlockSpec(memory_space=pl.ANY)
    return pl.pallas_call(
        sum_body,
        in_specs=[pl.BlockSpec(memory_space=pltpu.VMEM), anywhere],
        out_specs=anywhere,
        scratch_shapes=[
            pltpu.VMEM((back.shape[0], TRAILER, HEAD_DIM), BF),
            pltpu.SemaphoreType.DMA,
        ],
        out_shape=jax.ShapeDtypeStruct(back.shape, back.dtype),
        input_output_aliases={1: 0},
        compiler_params=VMEM,
        name="sum_taps",
    )(shares, back)


def shifted(block, steps):
    count = lax.axis_size("seq")
    return lax.ppermute(block, "seq", [(i, (i + steps) % count) for i in range(count)])


def with_neighbours(lattice, forward, place, ready=None):
    row_band, slab_index, col_half, band_count = place
    half = lax.axis_size("seq") // 2
    own = lattice.astype(BF)
    edge = jnp.where(col_half == 0, own[:, :, -1:], own[:, :, :1])
    frames = slice(-2, None) if forward else slice(0, 2)
    steps = band_count if forward else -band_count
    has_slab = slab_index > 0 if forward else slab_index < SLABS - 1
    own_edge = shifted(edge, half)
    near = shifted(own[frames], steps)
    near_edge = shifted(edge[frames], steps + half)
    near = jnp.where(has_slab, near, jnp.zeros_like(near)).astype(lattice.dtype)
    near_edge = jnp.where(has_slab, near_edge, jnp.zeros_like(near_edge))
    order = (lambda a, b: [a, b]) if forward else (lambda a, b: [b, a])
    middle = jnp.concatenate(order(near, lattice), axis=0)
    edges = jnp.concatenate(order(near_edge, own_edge), axis=0).astype(lattice.dtype)
    wide = side_columns(middle, edges, col_half)
    top, bottom = wide[:, :1].astype(BF), wide[:, -1:].astype(BF)
    if ready is not None:
        top, bottom = lax.optimization_barrier((top, bottom, ready))[:2]
    above = shifted(bottom, 1)
    below = shifted(top, -1)
    above = jnp.where(row_band > 0, above, jnp.zeros_like(above)).astype(lattice.dtype)
    below = jnp.where(row_band < band_count - 1, below, jnp.zeros_like(below))
    return jnp.concatenate([above, wide, below.astype(lattice.dtype)], axis=1)


def to_lattice(tokens):
    channels = tokens.shape[1]
    cube_count = tokens.shape[0] // 64
    lattice = tokens.reshape(cube_count, 4, 4, 4, channels).transpose(1, 2, 0, 3, 4)
    return lattice.reshape(4, 4, cube_count * 4, channels)


def from_lattice(lattice):
    channels = lattice.shape[3]
    cube_count = lattice.shape[2] // 4
    tokens = lattice.reshape(4, 4, cube_count, 4, channels).transpose(2, 0, 1, 3, 4)
    return tokens.reshape(cube_count * 64, channels)


def side_columns(lattice, edge, col_half):
    blank = jnp.zeros_like(edge)
    return jnp.concatenate(
        [jnp.where(col_half == 1, edge, blank), lattice, jnp.where(col_half == 0, edge, blank)],
        axis=2,
    )


def convolve_values(framed, filter_taps):
    frames = framed.shape[0] - 2
    height = framed.shape[1] - 2
    breadth = framed.shape[2] - 2
    totaled_sum = jnp.zeros((frames, height, breadth, framed.shape[3]), jnp.float32)
    for back_step in range(3):
        for row_step in (-1, 0, 1):
            for col_step in (-1, 0, 1):
                tap_index = back_step * 9 + (row_step + 1) * 3 + col_step + 1
                shifted = framed[
                    2 - back_step : 2 - back_step + frames,
                    1 + row_step : 1 + row_step + height,
                    1 + col_step : 1 + col_step + breadth,
                ]
                totaled_sum = totaled_sum + filter_taps[tap_index] * shifted.astype(jnp.float32)
    return totaled_sum


def convolve_back(grad_space, filter_taps):
    frames = grad_space.shape[0] - 2
    height = grad_space.shape[1] - 2
    breadth = grad_space.shape[2] - 2
    total = jnp.zeros((frames, height, breadth, grad_space.shape[3]), F32)
    for back_step in range(3):
        for row_step in (-1, 0, 1):
            for col_step in (-1, 0, 1):
                tap_index = back_step * 9 + (row_step + 1) * 3 + col_step + 1
                total = total + filter_taps[tap_index] * grad_space[
                    back_step : back_step + frames,
                    1 - row_step : 1 - row_step + height,
                    1 - col_step : 1 - col_step + breadth,
                ]
    return total


def pool_cubes(tokens):
    return jnp.mean(
        tokens.astype(jnp.float32).reshape(tokens.shape[0] // 64, 64, tokens.shape[1]), axis=1
    )


def spread(per_cube):
    cube_count = per_cube.shape[0]
    return jnp.broadcast_to(per_cube[:, None, :], (cube_count, 64, per_cube.shape[1])).reshape(
        cube_count * 64, per_cube.shape[1]
    )


def exchanged(rows):
    return lax.all_to_all(rows, "seq", split_axis=0, concat_axis=0, tiled=True)


def together(*values):
    return lax.optimization_barrier(values)


def shards(query_tokens, key_tokens, value_tokens, gate_tokens, filter_taps, selected, cotangent):
    devices = lax.axis_size("seq")
    device_index = lax.axis_index("seq")
    cube_count = query_tokens.shape[0] // 64
    pair_count = cube_count * HEADS
    channels = HEADS * HEAD_DIM
    capacity = max(3, 2 * HEADS * POOL // (devices - 1))
    logit_scale = HEAD_DIM ** (-0.5)
    band_count = devices // (2 * SLABS)
    rotated = (device_index + 2 * band_count + band_count // 2) % devices
    row_band = rotated % band_count
    slab_index = rotated // band_count % SLABS
    col_half = rotated // (devices // 2)

    owner_device = selected // cube_count
    pair_index = selected % cube_count * HEADS + jnp.arange(HEADS, dtype=jnp.int32)[None, :, None]
    owner_flat, pair_flat = owner_device.reshape(-1), pair_index.reshape(-1)
    remote_flat = owner_flat != device_index
    of_owner = (owner_flat[:, None] == jnp.arange(devices, dtype=jnp.int32)) & remote_flat[:, None]
    of_owner = of_owner.astype(BF)
    pair_ids = jnp.arange(pair_count, dtype=jnp.int32)
    of_pair = (pair_flat[:, None] == pair_ids).astype(BF)
    present = mm(of_owner, of_pair, ((0,), (0,))) > 0.5
    earlier = (pair_ids[:, None] < pair_ids).astype(BF)
    slot_rank = mm(present.astype(BF), earlier, ((1,), (0,)))
    in_slot = (slot_rank[:, None, :] == jnp.arange(capacity, dtype=F32)[None, :, None]) & (
        present[:, None, :]
    )
    requests = jnp.sum(jnp.where(in_slot, pair_ids, 0), axis=2).reshape(-1)
    asked_pairs = exchanged(requests)
    owner_rank = mm(of_owner, slot_rank.astype(BF), ((1,), (0,)))
    slot_of = jnp.sum(owner_rank * of_pair.astype(F32), axis=1).astype(jnp.int32)
    table_row = jnp.where(
        remote_flat, pair_count + owner_flat * capacity + slot_of, pair_flat
    )

    place = (row_band, slab_index, col_half, band_count)
    framed = with_neighbours(to_lattice(value_tokens), True, place, asked_pairs)

    asked_keys, framed = together(gather_pairs(asked_pairs, key_tokens, devices), framed)
    far_keys = exchanged(asked_keys)

    filtered = from_lattice(convolve_values(framed, filter_taps)).astype(BF)
    gated = cotangent.astype(F32) * gate_tokens.astype(F32)
    pooled = jnp.stack(
        [
            pool_cubes(query_tokens).astype(BF),
            pool_cubes(key_tokens).astype(BF),
            jnp.sum(gated.reshape(cube_count, 64, channels), axis=1).astype(BF),
            pool_cubes(filtered).astype(BF),
        ],
        axis=1,
    )
    pooled = pooled.reshape(cube_count, 4, HEADS, HEAD_DIM).transpose(2, 1, 0, 3)
    pooled = pooled.reshape(HEADS, 4 * cube_count, HEAD_DIM)
    asked_values, far_keys = together(
        gather_pairs(asked_pairs, filtered, devices, pooled), far_keys
    )
    far_values = exchanged(asked_values)
    one_head = far_values[:, capacity * 64 :].reshape(devices, 4, cube_count, HEAD_DIM)
    one_head = one_head.transpose(1, 0, 2, 3).reshape(4, devices * cube_count, HEAD_DIM)

    weights, own_value, back_value = fine_probs(
        table_row, query_tokens, cotangent, key_tokens, far_keys, capacity, logit_scale
    )
    block = (device_index // HEADS).reshape(1)
    back_value = exchanged(coarse_head(block, tuple(one_head), back_value, logit_scale))
    fine_out, fine_query, own_key, back_key = fine_grads(
        table_row, query_tokens, cotangent, key_tokens, far_keys, filtered, far_values, weights,
        capacity, logit_scale,
    )
    coarse = from_halves(back_value).reshape(cube_count, HEADS, 4, HEAD_DIM)
    coarse = coarse.transpose(2, 0, 1, 3).reshape(4, cube_count, channels)
    coarse_out, coarse_query = coarse[:2]

    coarse_tokens = spread(coarse_out)
    attended = (fine_out + gate_tokens.astype(F32) * coarse_tokens).astype(BF)
    gate_gradient = (cotangent.astype(F32) * coarse_tokens).astype(BF)
    query_gradient = (fine_query + spread(coarse_query) / 64.0).astype(BF)

    own_value, back_key = together(own_value, back_key)
    grad_lattice = collect(asked_pairs, own_value, back_value, back_value, 3, True)
    grad_space = with_neighbours(grad_lattice, False, place)
    shares = exchanged(tap_gradients(grad_lattice, framed).reshape(devices, TRAILER // 2, HEAD_DIM))
    back_key, grad_space = together(sum_taps(shares, back_key), grad_space)
    back_key = exchanged(back_key)
    taps = from_halves(back_key).reshape(8, HEADS, TRAILER // 2, HEAD_DIM)
    taps = taps.transpose(0, 2, 1, 3).reshape(-1, channels)
    filter_gradient = taps[: filter_taps.shape[0]]
    value_gradient = from_lattice(convolve_back(grad_space, filter_taps)).astype(BF)
    key_gradient = collect(asked_pairs, own_key, back_key, back_value, 2, False)
    return (attended, query_gradient, key_gradient, value_gradient, gate_gradient, filter_gradient)


def solution(mesh):
    return jax.shard_map(
        shards,
        mesh=mesh,
        in_specs=(
            P(("dp", "seq"), None),
            P(("dp", "seq"), None),
            P(("dp", "seq"), None),
            P(("dp", "seq"), None),
            P(),
            P(("dp", "seq"), None, None),
            P(("dp", "seq"), None),
        ),
        out_specs=(
            P(("dp", "seq"), None),
            P(("dp", "seq"), None),
            P(("dp", "seq"), None),
            P(("dp", "seq"), None),
            P(("dp", "seq"), None),
            P("dp", None),
        ),
        check_vma=False,
    )
```

```python
import functools
import jax
import jax.numpy as jnp
from jax import lax
from jax.experimental import pallas as pl
from jax.experimental.pallas import tpu as pltpu
from jax.sharding import PartitionSpec as P

HEAD_DIM = 128
HEADS = 8
SLABS = 4
POOL = 12
BF = jnp.bfloat16
F32 = jnp.float32
TRAILER = 8
VMEM = pltpu.CompilerParams(vmem_limit_bytes=56 << 20)


def head_lanes(h):
    if isinstance(h, int):
        return slice(h * HEAD_DIM, (h + 1) * HEAD_DIM)
    return pl.ds(pl.multiple_of(h * HEAD_DIM, HEAD_DIM), HEAD_DIM)


def cube_rows(c):
    if isinstance(c, int):
        return slice(c * 64, c * 64 + 64)
    return pl.ds(pl.multiple_of(c * 64, 64), 64)


def mm(a, b, dims):
    return lax.dot_general(a, b, (dims, ((), ())), preferred_element_type=F32)


def whole(shape):
    zeros = (0,) * len(shape)
    return pl.BlockSpec(shape, lambda *_: zeros)


def gather_body(pairs, tokens, *rest, dests, slots):
    extra, out = rest if len(rest) == 2 else (None, rest[0])
    base = pl.program_id(0) * dests

    def one(d, carry):
        for s in range(slots):
            p = pairs[(base + d) * slots + s]
            out[d, cube_rows(s)] = tokens[cube_rows(p // HEADS), head_lanes(p % HEADS)]
        if extra is not None:
            out[d, slots * 64 :] = extra[d % HEADS]
        return carry

    lax.fori_loop(0, dests, one, 0)


def gather_pairs(pairs, tokens, devices, extra=None):
    slots = pairs.shape[0] // devices
    dests = devices // 4
    rows = slots * 64 + (0 if extra is None else extra.shape[1])
    operands = (tokens,) if extra is None else (tokens, extra)
    return pl.pallas_call(
        functools.partial(gather_body, dests=dests, slots=slots),
        grid_spec=pltpu.PrefetchScalarGridSpec(
            num_scalar_prefetch=1,
            grid=(4,),
            in_specs=[whole(x.shape) for x in operands],
            out_specs=pl.BlockSpec((dests, rows, HEAD_DIM), lambda i, *_: (i, 0, 0)),
        ),
        out_shape=jax.ShapeDtypeStruct((devices, rows, HEAD_DIM), tokens.dtype),
        compiler_params=VMEM,
        name="gather_pairs",
    )(pairs, *operands)


def fill_table(table, tokens, fetched, pairs, slots):
    def near(p, carry):
        table[p] = tokens[cube_rows(p // HEADS), head_lanes(p % HEADS)]
        return carry

    lax.fori_loop(0, pairs, near, 0)

    def one(d, carry):
        for s in range(slots):
            table[pairs + d * slots + s] = fetched[d, cube_rows(s)]
        return carry

    lax.fori_loop(0, fetched.shape[0], one, 0)


def clear(acc):
    def one(i, carry):
        acc[i] = jnp.zeros(acc.shape[1:], acc.dtype)
        return carry

    lax.fori_loop(0, acc.shape[0], one, 0, unroll=2)


def flush(acc, own, far, pairs, slots):
    def near(i, carry):
        own[i] = acc[i]
        return carry

    def distant(d, carry):
        for s in range(slots):
            far[d, cube_rows(s)] = acc[pairs + d * slots + s].astype(far.dtype)
        if far.shape[1] > slots * 64:
            far[d, slots * 64 :] = jnp.zeros((TRAILER, HEAD_DIM), far.dtype)
        return carry

    lax.fori_loop(0, pairs, near, 0)
    lax.fori_loop(0, far.shape[0], distant, 0)


def picked(rows, cube, h):
    return [rows[(cube * HEADS + h) * 8 + i] for i in range(8)]


def probs_body(rows, query, grad, keys, far_keys, weights, own, far, table, acc, *, scale, pairs, slots):
    cube = pl.program_id(0)

    @pl.when(cube == 0)
    def _():
        fill_table(table, keys, far_keys, pairs, slots)
        clear(acc)

    def one_head(h):
        lanes = head_lanes(h)
        rs = picked(rows, cube, h)
        key_rows = jnp.concatenate([table[r] for r in rs], axis=0)
        logits = mm(query[:, lanes], key_rows, ((1,), (1,))) * scale
        expo = jnp.exp(logits - jnp.max(logits, axis=1, keepdims=True))
        w = expo / jnp.sum(expo, axis=1, keepdims=True)
        weights[h] = w
        part = mm(w.astype(BF), grad[:, lanes], ((0,), (0,)))
        for i, r in enumerate(rs):
            acc[r] += part[64 * i : 64 * i + 64]

    def two_heads(i, carry):
        one_head(2 * i)
        one_head(2 * i + 1)
        return carry

    lax.fori_loop(0, HEADS // 2, two_heads, 0)

    @pl.when(cube == pl.num_programs(0) - 1)
    def _():
        flush(acc, own, far, pairs, slots)


def fine_probs(rows, query, grad, keys, far_keys, slots, scale):
    cubes = query.shape[0] // 64
    pairs = cubes * HEADS
    devices = far_keys.shape[0]
    far_shape = (devices, slots * 64 + TRAILER, HEAD_DIM)
    width = HEADS * HEAD_DIM
    cube_block = pl.BlockSpec((64, width), lambda c, *_: (c, 0))
    return pl.pallas_call(
        functools.partial(probs_body, scale=scale, pairs=pairs, slots=slots),
        grid_spec=pltpu.PrefetchScalarGridSpec(
            num_scalar_prefetch=1,
            grid=(cubes,),
            in_specs=[cube_block, cube_block, whole(keys.shape), whole(far_keys.shape)],
            out_specs=[
                pl.BlockSpec((HEADS, 64, 512), lambda c, *_: (c, 0, 0)),
                whole((pairs, 64, HEAD_DIM)),
                whole(far_shape),
            ],
            scratch_shapes=[
                pltpu.VMEM((pairs + devices * slots, 64, HEAD_DIM), BF),
                pltpu.VMEM((pairs + devices * slots, 64, HEAD_DIM), F32),
            ],
        ),
        out_shape=[
            jax.ShapeDtypeStruct((pairs, 64, 512), F32),
            jax.ShapeDtypeStruct((pairs, 64, HEAD_DIM), F32),
            jax.ShapeDtypeStruct(far_shape, BF),
        ],
        compiler_params=VMEM,
        name="fine_probs",
    )(rows, query, grad, keys, far_keys)


def grads_body(
    rows, query, grad, keys, far_keys, values, far_values, weights,
    fine_out, fine_query, own, far, key_table, value_table, acc, *, scale, pairs, slots,
):
    cube = pl.program_id(0)

    @pl.when(cube == 0)
    def _():
        fill_table(key_table, keys, far_keys, pairs, slots)
        fill_table(value_table, values, far_values, pairs, slots)
        clear(acc)

    def one_head(h):
        lanes = head_lanes(h)
        rs = picked(rows, cube, h)
        key_rows = jnp.concatenate([key_table[r] for r in rs], axis=0)
        value_rows = jnp.concatenate([value_table[r] for r in rs], axis=0)
        g = grad[:, lanes]
        w = weights[h]
        out = mm(w.astype(BF), value_rows, ((1,), (0,)))
        delta = jnp.sum(g.astype(F32) * out, axis=1, keepdims=True)
        slope = mm(g, value_rows, ((1,), (1,)))
        ds = (w * (slope - delta)).astype(BF)
        fine_out[:, lanes] = out
        fine_query[:, lanes] = mm(ds, key_rows, ((1,), (0,))) * scale
        part = mm(ds, query[:, lanes], ((0,), (0,))) * scale
        for i, r in enumerate(rs):
            acc[r] += part[64 * i : 64 * i + 64]

    def two_heads(i, carry):
        one_head(2 * i)
        one_head(2 * i + 1)
        return carry

    lax.fori_loop(0, HEADS // 2, two_heads, 0)

    @pl.when(cube == pl.num_programs(0) - 1)
    def _():
        flush(acc, own, far, pairs, slots)


def fine_grads(rows, query, grad, keys, far_keys, values, far_values, weights, slots, scale):
    cubes = query.shape[0] // 64
    pairs = cubes * HEADS
    devices = far_keys.shape[0]
    far_shape = (devices, slots * 64, HEAD_DIM)
    width = HEADS * HEAD_DIM
    cube_block = pl.BlockSpec((64, width), lambda c, *_: (c, 0))
    table = (pairs + devices * slots, 64, HEAD_DIM)
    return pl.pallas_call(
        functools.partial(grads_body, scale=scale, pairs=pairs, slots=slots),
        grid_spec=pltpu.PrefetchScalarGridSpec(
            num_scalar_prefetch=1,
            grid=(cubes,),
            in_specs=[
                cube_block,
                cube_block,
                whole(keys.shape),
                whole(far_keys.shape),
                whole(values.shape),
                whole(far_values.shape),
                pl.BlockSpec((HEADS, 64, 512), lambda c, *_: (c, 0, 0)),
            ],
            out_specs=[
                cube_block,
                cube_block,
                whole((pairs, 64, HEAD_DIM)),
                whole(far_shape),
            ],
            scratch_shapes=[
                pltpu.VMEM(table, BF),
                pltpu.VMEM(table, BF),
                pltpu.VMEM(table, F32),
            ],
        ),
        out_shape=[
            jax.ShapeDtypeStruct(query.shape, F32),
            jax.ShapeDtypeStruct(query.shape, F32),
            jax.ShapeDtypeStruct((pairs, 64, HEAD_DIM), F32),
            jax.ShapeDtypeStruct(far_shape, BF),
        ],
        compiler_params=VMEM,
        name="fine_grads",
    )(rows, query, grad, keys, far_keys, values, far_values, weights)


def add_returned(pairs, own, back, trailer, acc, quantity):
    slots = pairs.shape[0] // back.shape[0]
    for p in range(own.shape[0]):
        c, h = p // HEADS, p % HEADS
        high = trailer[p, quantity : quantity + 1].astype(F32)
        low = trailer[p, TRAILER // 2 + quantity : TRAILER // 2 + quantity + 1].astype(F32)
        acc[cube_rows(c), head_lanes(h)] = own[p] + (high + low) * (1.0 / 64.0)

    def one(d, carry):
        for s in range(slots):
            p = pairs[d * slots + s]
            rows = cube_rows(p // HEADS)
            lanes = head_lanes(p % HEADS)
            acc[rows, lanes] += back[d, cube_rows(s)].astype(F32)
        return carry

    lax.fori_loop(0, back.shape[0], one, 0)


def collect_keys_body(pairs, own, back, trailer, out, acc):
    add_returned(pairs, own, back, trailer, acc, 2)
    out[...] = acc[...].astype(out.dtype)


PIECES = (
    (256, (0, 1, 0)),
    (16, (0, 0, 1)),
    (8, (0, 1, 1)),
    (128, (1, 0, 0)),
    (64, (1, 1, 0)),
    (8, (1, 0, 1)),
    (8, (1, 1, 1)),
    (128, (-1, 0, 0)),
    (64, (-1, 1, 0)),
    (8, (-1, 0, 1)),
    (8, (-1, 1, 1)),
)


def collect_values_body(pairs, half, own, back, trailer, out, *rest):
    pieces, acc = rest[:-1], rest[-1]
    add_returned(pairs, own, back, trailer, acc, 3)

    def lane_block(h, carry):
        lanes = head_lanes(h)
        for g in range(acc.shape[0] // 64):
            for i in range(16):
                row = 64 * g + 4 * i
                out[i // 4, i % 4, 4 * g : 4 * g + 4, lanes] = acc[row : row + 4, lanes]
        near, edge, near_edge = pieces[:3]
        for i in range(8):
            near[32 * i : 32 * i + 32, lanes] = out[i // 4, i % 4, :, lanes].astype(BF)
        column = jnp.concatenate(
            [
                jnp.where(
                    half[0] == 0,
                    out[i // 4, i % 4, 31:32, lanes],
                    out[i // 4, i % 4, 0:1, lanes],
                )
                for i in range(16)
            ],
            axis=0,
        )
        edge[:, lanes] = column.astype(BF)
        near_edge[:, lanes] = column[0:8].astype(BF)
        blank = jnp.zeros((1, HEAD_DIM), F32)
        for y, (row, near_row, corner, near_corner) in ((3, pieces[3:7]), (0, pieces[7:11])):
            for t in range(4):
                cells = out[t, y, :, lanes].astype(BF)
                row[32 * t : 32 * t + 32, lanes] = cells
                if t < 2:
                    near_row[32 * t : 32 * t + 32, lanes] = cells
            picks = [column[4 * t + y : 4 * t + y + 1] for t in range(4)]
            corner[:, lanes] = jnp.concatenate(picks + [blank] * 4, axis=0).astype(BF)
            near_corner[:, lanes] = jnp.concatenate(picks[:2] + [blank] * 6, axis=0).astype(BF)
        return carry

    lax.fori_loop(0, HEADS, lane_block, 0)


def collect(pairs, own, back, halves, half=None):
    cubes = own.shape[0] // HEADS
    width = HEADS * HEAD_DIM
    tokens = (cubes * 64, width)
    last = halves.shape[1] // TRAILER - 1
    if half is None:
        scalars, body = (pairs,), collect_keys_body
        shapes = [jax.ShapeDtypeStruct(tokens, BF)]
    else:
        scalars, body = (pairs, half), collect_values_body
        shapes = [jax.ShapeDtypeStruct((4, 4, 4 * cubes, width), F32)]
        shapes += [jax.ShapeDtypeStruct((rows, width), BF) for rows, _ in PIECES]
    return pl.pallas_call(
        body,
        grid_spec=pltpu.PrefetchScalarGridSpec(
            num_scalar_prefetch=len(scalars),
            grid=(1,),
            in_specs=[
                whole(own.shape),
                whole(back.shape),
                pl.BlockSpec((halves.shape[0], TRAILER, HEAD_DIM), lambda *_: (0, last, 0)),
            ],
            out_specs=[whole(x.shape) for x in shapes],
            scratch_shapes=[pltpu.VMEM(tokens, F32)],
        ),
        out_shape=shapes,
        compiler_params=VMEM,
        name="collect",
    )(*scalars, own, back, halves)


def put_tokens(out, sums, tokens):
    for i in range(16):
        for g in range(tokens.shape[0] // 64):
            row = 64 * g + 4 * i
            tokens[row : row + 4] = sums[i, 4 * g : 4 * g + 4]
    out[...] = tokens[...].astype(out.dtype)


def forward_body(framed, taps, out, wide, left, middle, right, sums, tokens):
    for p in range(36):
        wide[p, 0:34] = framed[p // 6, p % 6].astype(F32)
        left[p] = wide[p, 0:32]
        middle[p] = wide[p, 1:33]
        right[p] = wide[p, 2:34]

    def one(i, carry):
        f, y = i // 4, i % 4
        total = jnp.zeros((32, HEAD_DIM), F32)
        for back in range(3):
            for row in (-1, 0, 1):
                plane = (f + 2 - back) * 6 + y + 1 + row
                for col, cells in ((-1, left), (0, middle), (1, right)):
                    tap = 9 * back + 3 * (row + 1) + col + 1
                    total = total + taps[tap : tap + 1] * cells[plane]
        sums[i] = total
        return carry

    lax.fori_loop(0, 16, one, 0)
    put_tokens(out, sums, tokens)


def filter_forward(framed, taps):
    planes = framed.shape[0] * framed.shape[1]
    breadth, width = framed.shape[2] - 2, framed.shape[3]
    rows = 16 * breadth
    return pl.pallas_call(
        forward_body,
        grid=(HEADS,),
        in_specs=[
            pl.BlockSpec(framed.shape[:3] + (HEAD_DIM,), lambda i: (0, 0, 0, i)),
            pl.BlockSpec((taps.shape[0], HEAD_DIM), lambda i: (0, i)),
        ],
        out_specs=pl.BlockSpec((rows, HEAD_DIM), lambda i: (0, i)),
        scratch_shapes=[pltpu.VMEM((planes, 40, HEAD_DIM), F32)]
        + [pltpu.VMEM((planes, breadth, HEAD_DIM), F32)] * 3
        + [pltpu.VMEM((16, breadth, HEAD_DIM), F32), pltpu.VMEM((rows, HEAD_DIM), F32)],
        out_shape=jax.ShapeDtypeStruct((rows, width), BF),
        compiler_params=VMEM,
        name="filter_forward",
    )(framed, taps)


def back_body(flags, grad, *rest):
    pieces = rest[: len(PIECES)]
    taps, out, wide, left, middle, right, sums, tokens = rest[len(PIECES) :]
    near, edge, near_edge = pieces[:3]
    half = flags[0]
    small = [pieces[i][...].astype(F32) for i in (1, 2, 5, 6, 9, 10)]
    edge, near_edge, top_edge, near_top_edge, low_edge, near_low_edge = small
    blank = jnp.zeros((1, HEAD_DIM), F32)
    for t in range(6):
        for r in range(6):
            p = 6 * t + r
            n = t - 4
            shown = None
            if 1 <= r <= 4:
                if t < 4:
                    cells, k, source = grad[t, r - 1], 4 * t + r - 1, edge
                else:
                    i = 4 * n + r - 1
                    cells, k, source = near[32 * i : 32 * i + 32].astype(F32), i, near_edge
                    shown = flags[1] > 0
            else:
                row, near_row = pieces[3:5] if r == 0 else pieces[7:9]
                shown = flags[2 if r == 0 else 3] > 0
                if t < 4:
                    cells, k = row[32 * t : 32 * t + 32].astype(F32), t
                    source = top_edge if r == 0 else low_edge
                else:
                    cells, k = near_row[32 * n : 32 * n + 32].astype(F32), n
                    source = near_top_edge if r == 0 else near_low_edge
                    shown = shown & (flags[1] > 0)
            side = source[k : k + 1]
            if shown is not None:
                cells = jnp.where(shown, cells, 0.0)
                side = jnp.where(shown, side, 0.0)
            wide[p, 8:40] = cells
            wide[p, 7:8] = jnp.where(half == 1, side, blank)
            wide[p, 40:41] = jnp.where(half == 0, side, blank)
            left[p] = wide[p, 7:39]
            middle[p] = cells
            right[p] = wide[p, 9:41]

    def one(i, carry):
        f, y = i // 4, i % 4
        total = jnp.zeros((32, HEAD_DIM), F32)
        for back in range(3):
            for row in (-1, 0, 1):
                plane = (f + back) * 6 + y + 1 - row
                for col, cells in ((-1, right), (0, middle), (1, left)):
                    tap = 9 * back + 3 * (row + 1) + col + 1
                    total = total + taps[tap : tap + 1] * cells[plane]
        sums[i] = total
        return carry

    lax.fori_loop(0, 16, one, 0)
    put_tokens(out, sums, tokens)


def filter_back(flags, grad, pieces, taps):
    frames, height, breadth, width = grad.shape
    rows = frames * height * breadth
    planes = (frames + 2) * (height + 2)
    return pl.pallas_call(
        back_body,
        grid_spec=pltpu.PrefetchScalarGridSpec(
            num_scalar_prefetch=1,
            grid=(HEADS,),
            in_specs=[pl.BlockSpec(grad.shape[:3] + (HEAD_DIM,), lambda i, *_: (0, 0, 0, i))]
            + [pl.BlockSpec((x.shape[0], HEAD_DIM), lambda i, *_: (0, i)) for x in (*pieces, taps)],
            out_specs=pl.BlockSpec((rows, HEAD_DIM), lambda i, *_: (0, i)),
            scratch_shapes=[pltpu.VMEM((planes, 48, HEAD_DIM), F32)]
            + [pltpu.VMEM((planes, breadth, HEAD_DIM), F32)] * 3
            + [
                pltpu.VMEM((frames * height, breadth, HEAD_DIM), F32),
                pltpu.VMEM((rows, HEAD_DIM), F32),
            ],
        ),
        out_shape=jax.ShapeDtypeStruct((rows, width), BF),
        compiler_params=VMEM,
        name="filter_back",
    )(flags, grad, *pieces, taps)


def put_halves(target, sem, stage, parts):
    for i, part in enumerate(parts):
        high = part.astype(BF)
        stage[:, i] = high
        stage[:, len(parts) + i] = (part - high.astype(F32)).astype(BF)
    rows = target.shape[1]
    copy = pltpu.make_async_copy(
        stage, target.at[:, pl.ds(rows - TRAILER, TRAILER)], sem
    )
    copy.start()
    copy.wait()


def from_halves(received):
    halves = received[:, -TRAILER:].astype(F32)
    return halves[:, : TRAILER // 2] + halves[:, TRAILER // 2 :]


def coarse_body(block, query, key, grad, value, back, out, stage, sem, *, scale):
    del back
    q, k, g, v = query[...], key[...], grad[...], value[...]
    logits = mm(k, q, ((1,), (1,))) * scale
    expo = jnp.exp(logits - jnp.max(logits, axis=0, keepdims=True))
    w = expo / jnp.sum(expo, axis=0, keepdims=True)
    wr = w.astype(BF)
    slope = mm(v, g, ((1,), (1,)))
    delta = jnp.sum(wr.astype(F32) * slope, axis=0, keepdims=True)
    ds = (w * (slope - delta)).astype(BF)
    results = (
        mm(wr, v, ((0,), (0,))),
        mm(ds, k, ((0,), (0,))) * scale,
        mm(ds, q, ((1,), (0,))) * scale,
        mm(wr, g, ((1,), (0,))),
    )
    shape = (results[0].shape[0] // 8, 8, HEAD_DIM)
    mine = lax.broadcasted_iota(jnp.int32, shape, 1) == block[0]
    parts = [jnp.sum(jnp.where(mine, r.reshape(shape), 0.0), axis=1) for r in results]
    put_halves(out, sem, stage, parts)


def coarse_head(block, pooled, back, scale):
    anywhere = pl.BlockSpec(memory_space=pl.ANY)
    return pl.pallas_call(
        functools.partial(coarse_body, scale=scale),
        grid_spec=pltpu.PrefetchScalarGridSpec(
            num_scalar_prefetch=1,
            grid=(1,),
            in_specs=[whole(x.shape) for x in pooled] + [anywhere],
            out_specs=anywhere,
            scratch_shapes=[
                pltpu.VMEM((back.shape[0], TRAILER, HEAD_DIM), BF),
                pltpu.SemaphoreType.DMA,
            ],
        ),
        out_shape=jax.ShapeDtypeStruct(back.shape, back.dtype),
        input_output_aliases={5: 0},
        compiler_params=VMEM,
        name="coarse_head",
    )(block, *pooled, back)


def taps_body(member, grad, framed, out, wide):
    del member
    frames, height, breadth = grad.shape[:3]
    planes, rows = framed.shape[:2]
    for t in range(planes):
        for r in range(rows):
            wide[t * rows + r, 0 : framed.shape[2]] = framed[t, r].astype(F32)
    for col in range(3):
        sums = {}
        for t in range(planes):
            for r in range(rows):
                cells = wide[t * rows + r, col : col + breadth]
                for back in range(3):
                    for row in range(3):
                        f, y = t - 2 + back, r - row
                        if 0 <= f < frames and 0 <= y < height:
                            tap = 9 * back + 3 * row + col
                            term = jnp.sum((grad[f, y] * cells).reshape(-1, 8, 128), axis=0)
                            sums[tap] = sums[tap] + term if tap in sums else term
        for tap, total in sums.items():
            out[0, tap : tap + 1] = jnp.sum(total, axis=0, keepdims=True)
    out[0, 27:] = jnp.zeros((5, 128), F32)


def tap_gradients(member, grad, framed):
    return pl.pallas_call(
        taps_body,
        grid_spec=pltpu.PrefetchScalarGridSpec(
            num_scalar_prefetch=1,
            grid=(HEADS,),
            in_specs=[
                pl.BlockSpec(grad.shape[:3] + (128,), lambda i, m: (0, 0, 0, i)),
                pl.BlockSpec(framed.shape[:3] + (128,), lambda i, m: (0, 0, 0, i)),
            ],
            out_specs=pl.BlockSpec(
                (1, 32, 128), lambda i, m: ((i + HEADS - m[0]) % HEADS, 0, 0)
            ),
            scratch_shapes=[pltpu.VMEM((framed.shape[0] * framed.shape[1], 40, 128), F32)],
        ),
        out_shape=jax.ShapeDtypeStruct((HEADS, 32, 128), F32),
        compiler_params=VMEM,
        name="tap_gradients",
    )(member, grad, framed)


def shifted(block, steps):
    count = lax.axis_size("seq")
    return lax.ppermute(block, "seq", [(i, (i + steps) % count) for i in range(count)])


def with_neighbours(lattice, forward, place, ready=None):
    row_band, slab_index, col_half, band_count = place
    half = lax.axis_size("seq") // 2
    own = lattice.astype(BF)
    edge = jnp.where(col_half == 0, own[:, :, -1:], own[:, :, :1])
    frames = slice(-2, None) if forward else slice(0, 2)
    steps = band_count if forward else -band_count
    has_slab = slab_index > 0 if forward else slab_index < SLABS - 1
    own_edge = shifted(edge, half)
    near = shifted(own[frames], steps)
    near_edge = shifted(edge[frames], steps + half)
    near = jnp.where(has_slab, near, jnp.zeros_like(near)).astype(lattice.dtype)
    near_edge = jnp.where(has_slab, near_edge, jnp.zeros_like(near_edge))
    order = (lambda a, b: [a, b]) if forward else (lambda a, b: [b, a])
    middle = jnp.concatenate(order(near, lattice), axis=0)
    edges = jnp.concatenate(order(near_edge, own_edge), axis=0).astype(lattice.dtype)
    wide = side_columns(middle, edges, col_half)
    top, bottom = wide[:, :1].astype(BF), wide[:, -1:].astype(BF)
    if ready is not None:
        top, bottom = lax.optimization_barrier((top, bottom, ready))[:2]
    above = shifted(bottom, 1)
    below = shifted(top, -1)
    above = jnp.where(row_band > 0, above, jnp.zeros_like(above)).astype(lattice.dtype)
    below = jnp.where(row_band < band_count - 1, below, jnp.zeros_like(below))
    return jnp.concatenate([above, wide, below.astype(lattice.dtype)], axis=1)


def to_lattice(tokens):
    channels = tokens.shape[1]
    cube_count = tokens.shape[0] // 64
    lattice = tokens.reshape(cube_count, 4, 4, 4, channels).transpose(1, 2, 0, 3, 4)
    return lattice.reshape(4, 4, cube_count * 4, channels)


def side_columns(lattice, edge, col_half):
    blank = jnp.zeros_like(edge)
    return jnp.concatenate(
        [jnp.where(col_half == 1, edge, blank), lattice, jnp.where(col_half == 0, edge, blank)],
        axis=2,
    )


def pool_cubes(tokens):
    return jnp.mean(
        tokens.astype(jnp.float32).reshape(tokens.shape[0] // 64, 64, tokens.shape[1]), axis=1
    )


def spread(per_cube):
    cube_count = per_cube.shape[0]
    return jnp.broadcast_to(per_cube[:, None, :], (cube_count, 64, per_cube.shape[1])).reshape(
        cube_count * 64, per_cube.shape[1]
    )


def exchanged(rows, groups=None):
    return lax.all_to_all(
        rows, "seq", split_axis=0, concat_axis=0, tiled=True, axis_index_groups=groups
    )


def in_plane(block, ahead):
    count = lax.axis_size("seq")
    return lax.ppermute(
        block, "seq", [(i, i // HEADS * HEADS + (i + ahead) % HEADS) for i in range(count)]
    )


def together(*values):
    return lax.optimization_barrier(values)


def shards(query_tokens, key_tokens, value_tokens, gate_tokens, filter_taps, selected, cotangent):
    devices = lax.axis_size("seq")
    device_index = lax.axis_index("seq")
    cube_count = query_tokens.shape[0] // 64
    pair_count = cube_count * HEADS
    channels = HEADS * HEAD_DIM
    capacity = max(3, 2 * HEADS * POOL // (devices - 1))
    logit_scale = HEAD_DIM ** (-0.5)
    band_count = devices // (2 * SLABS)
    rotated = (device_index + 2 * band_count + band_count // 2) % devices
    row_band = rotated % band_count
    slab_index = rotated // band_count % SLABS
    col_half = rotated // (devices // 2)

    owner_device = selected // cube_count
    pair_index = selected % cube_count * HEADS + jnp.arange(HEADS, dtype=jnp.int32)[None, :, None]
    owner_flat, pair_flat = owner_device.reshape(-1), pair_index.reshape(-1)
    remote_flat = owner_flat != device_index
    of_owner = (owner_flat[:, None] == jnp.arange(devices, dtype=jnp.int32)) & remote_flat[:, None]
    of_owner = of_owner.astype(BF)
    pair_ids = jnp.arange(pair_count, dtype=jnp.int32)
    of_pair = (pair_flat[:, None] == pair_ids).astype(BF)
    present = mm(of_owner, of_pair, ((0,), (0,))) > 0.5
    earlier = (pair_ids[:, None] < pair_ids).astype(BF)
    slot_rank = mm(present.astype(BF), earlier, ((1,), (0,)))
    in_slot = (slot_rank[:, None, :] == jnp.arange(capacity, dtype=F32)[None, :, None]) & (
        present[:, None, :]
    )
    requests = jnp.sum(jnp.where(in_slot, pair_ids, 0), axis=2).reshape(-1)
    asked_pairs = exchanged(requests)
    owner_rank = mm(of_owner, slot_rank.astype(BF), ((1,), (0,)))
    slot_of = jnp.sum(owner_rank * of_pair.astype(F32), axis=1).astype(jnp.int32)
    table_row = jnp.where(
        remote_flat, pair_count + owner_flat * capacity + slot_of, pair_flat
    )

    place = (row_band, slab_index, col_half, band_count)
    framed = with_neighbours(to_lattice(value_tokens), True, place, asked_pairs)

    asked_keys, framed = together(gather_pairs(asked_pairs, key_tokens, devices), framed)
    far_keys = exchanged(asked_keys)

    filtered = filter_forward(framed, filter_taps)
    gated = cotangent.astype(F32) * gate_tokens.astype(F32)
    pooled = jnp.stack(
        [
            pool_cubes(query_tokens).astype(BF),
            pool_cubes(key_tokens).astype(BF),
            jnp.sum(gated.reshape(cube_count, 64, channels), axis=1).astype(BF),
            pool_cubes(filtered).astype(BF),
        ],
        axis=1,
    )
    pooled = pooled.reshape(cube_count, 4, HEADS, HEAD_DIM).transpose(2, 1, 0, 3)
    pooled = pooled.reshape(HEADS, 4 * cube_count, HEAD_DIM)
    asked_values, far_keys = together(
        gather_pairs(asked_pairs, filtered, devices, pooled), far_keys
    )
    far_values = exchanged(asked_values)
    one_head = far_values[:, capacity * 64 :].reshape(devices, 4, cube_count, HEAD_DIM)
    one_head = one_head.transpose(1, 0, 2, 3).reshape(4, devices * cube_count, HEAD_DIM)

    weights, own_value, back_value = fine_probs(
        table_row, query_tokens, cotangent, key_tokens, far_keys, capacity, logit_scale
    )
    block = (device_index // HEADS).reshape(1)
    back_value = exchanged(coarse_head(block, tuple(one_head), back_value, logit_scale))
    fine_out, fine_query, own_key, back_key = fine_grads(
        table_row, query_tokens, cotangent, key_tokens, far_keys, filtered, far_values, weights,
        capacity, logit_scale,
    )
    coarse = from_halves(back_value).reshape(cube_count, HEADS, 4, HEAD_DIM)
    coarse = coarse.transpose(2, 0, 1, 3).reshape(4, cube_count, channels)
    coarse_out, coarse_query = coarse[:2]

    coarse_tokens = spread(coarse_out)
    attended = (fine_out + gate_tokens.astype(F32) * coarse_tokens).astype(BF)
    gate_gradient = (cotangent.astype(F32) * coarse_tokens).astype(BF)
    query_gradient = (fine_query + spread(coarse_query) / 64.0).astype(BF)

    back_key, back_value = together(back_key, back_value)
    back_key = exchanged(back_key)
    grad_lattice, *pieces = collect(
        asked_pairs, own_value, back_value, back_value, col_half.reshape(1)
    )
    cells = [
        shifted(piece, rows - band_count * slabs + devices // 2 * halves)
        for piece, (_, (rows, slabs, halves)) in zip(pieces, PIECES)
    ]
    shares = tap_gradients((device_index % HEADS).reshape(1), grad_lattice, framed)
    mates = [in_plane(shares[ahead], ahead) for ahead in range(1, HEADS)]

    back_key, *arrived = together(back_key, *cells, *mates)
    cells, mates = arrived[: len(cells)], arrived[len(cells) :]
    taps = sum(mates, shares[0])
    rest = devices // HEADS
    columns = [[HEADS * b + h for b in range(rest)] for h in range(HEADS)]
    planes = [[HEADS * b + h for h in range(HEADS)] for b in range(rest)]
    taps = jnp.sum(exchanged(jnp.broadcast_to(taps[None], (rest, 32, 128)), columns), axis=0)
    taps = exchanged(jnp.broadcast_to(taps[None], (HEADS, 32, 128)), planes)
    filter_gradient = taps.transpose(1, 0, 2).reshape(32, channels)[: filter_taps.shape[0]]
    flags = jnp.stack(
        [
            col_half,
            (slab_index < SLABS - 1).astype(jnp.int32),
            (row_band > 0).astype(jnp.int32),
            (row_band < band_count - 1).astype(jnp.int32),
        ]
    )
    value_gradient = filter_back(flags, grad_lattice, cells, filter_taps)
    (key_gradient,) = collect(asked_pairs, own_key, back_key, back_value)
    return (attended, query_gradient, key_gradient, value_gradient, gate_gradient, filter_gradient)


def solution(mesh):
    return jax.shard_map(
        shards,
        mesh=mesh,
        in_specs=(
            P(("dp", "seq"), None),
            P(("dp", "seq"), None),
            P(("dp", "seq"), None),
            P(("dp", "seq"), None),
            P(),
            P(("dp", "seq"), None, None),
            P(("dp", "seq"), None),
        ),
        out_specs=(
            P(("dp", "seq"), None),
            P(("dp", "seq"), None),
            P(("dp", "seq"), None),
            P(("dp", "seq"), None),
            P(("dp", "seq"), None),
            P("dp", None),
        ),
        check_vma=False,
    )
```

```python
import functools
import jax
import jax.numpy as jnp
from jax import lax
from jax.experimental import pallas as pl
from jax.experimental.pallas import tpu as pltpu
from jax.sharding import PartitionSpec as P

HEAD_DIM = 128
HEADS = 8
SLABS = 4
POOL = 12
BF = jnp.bfloat16
F32 = jnp.float32
TRAILER = 8
VMEM = pltpu.CompilerParams(vmem_limit_bytes=56 << 20)


def head_lanes(h):
    if isinstance(h, int):
        return slice(h * HEAD_DIM, (h + 1) * HEAD_DIM)
    return pl.ds(pl.multiple_of(h * HEAD_DIM, HEAD_DIM), HEAD_DIM)


def cube_rows(c):
    if isinstance(c, int):
        return slice(c * 64, c * 64 + 64)
    return pl.ds(pl.multiple_of(c * 64, 64), 64)


def mm(a, b, dims):
    return lax.dot_general(a, b, (dims, ((), ())), preferred_element_type=F32)


def whole(shape):
    zeros = (0,) * len(shape)
    return pl.BlockSpec(shape, lambda *_: zeros)


def gather_body(pairs, tokens, *rest, dests, slots):
    extra, out = rest if len(rest) == 2 else (None, rest[0])
    base = pl.program_id(0) * dests

    def one(d, carry):
        for s in range(slots):
            p = pairs[(base + d) * slots + s]
            out[d, cube_rows(s)] = tokens[cube_rows(p // HEADS), head_lanes(p % HEADS)]
        if extra is not None:
            out[d, slots * 64 :] = extra[d % HEADS]
        return carry

    lax.fori_loop(0, dests, one, 0)


def gather_pairs(pairs, tokens, devices, extra=None):
    slots = pairs.shape[0] // devices
    dests = devices // 4
    rows = slots * 64 + (0 if extra is None else extra.shape[1])
    operands = (tokens,) if extra is None else (tokens, extra)
    return pl.pallas_call(
        functools.partial(gather_body, dests=dests, slots=slots),
        grid_spec=pltpu.PrefetchScalarGridSpec(
            num_scalar_prefetch=1,
            grid=(4,),
            in_specs=[whole(x.shape) for x in operands],
            out_specs=pl.BlockSpec((dests, rows, HEAD_DIM), lambda i, *_: (i, 0, 0)),
        ),
        out_shape=jax.ShapeDtypeStruct((devices, rows, HEAD_DIM), tokens.dtype),
        compiler_params=VMEM,
        name="gather_pairs",
    )(pairs, *operands)


def fill_table(table, tokens, fetched, pairs, slots):
    def near(p, carry):
        table[p] = tokens[cube_rows(p // HEADS), head_lanes(p % HEADS)]
        return carry

    lax.fori_loop(0, pairs, near, 0)

    def one(d, carry):
        for s in range(slots):
            table[pairs + d * slots + s] = fetched[d, cube_rows(s)]
        return carry

    lax.fori_loop(0, fetched.shape[0], one, 0)


def clear(acc):
    def one(i, carry):
        acc[i] = jnp.zeros(acc.shape[1:], acc.dtype)
        return carry

    lax.fori_loop(0, acc.shape[0], one, 0, unroll=2)


def flush(acc, own, far, pairs, slots):
    def near(i, carry):
        own[i] = acc[i]
        return carry

    def distant(d, carry):
        for s in range(slots):
            far[d, cube_rows(s)] = acc[pairs + d * slots + s].astype(far.dtype)
        if far.shape[1] > slots * 64:
            far[d, slots * 64 :] = jnp.zeros((TRAILER, HEAD_DIM), far.dtype)
        return carry

    lax.fori_loop(0, pairs, near, 0)
    lax.fori_loop(0, far.shape[0], distant, 0)


def picked(rows, cube, h):
    return [rows[(cube * HEADS + h) * 8 + i] for i in range(8)]


def probs_body(rows, query, grad, keys, far_keys, weights, own, far, table, acc, *, scale, pairs, slots):
    cube = pl.program_id(0)

    @pl.when(cube == 0)
    def _():
        fill_table(table, keys, far_keys, pairs, slots)
        clear(acc)

    def one_head(h):
        lanes = head_lanes(h)
        rs = picked(rows, cube, h)
        key_rows = jnp.concatenate([table[r] for r in rs], axis=0)
        logits = mm(query[:, lanes], key_rows, ((1,), (1,))) * scale
        expo = jnp.exp(logits - jnp.max(logits, axis=1, keepdims=True))
        w = expo / jnp.sum(expo, axis=1, keepdims=True)
        weights[h] = w
        part = mm(w.astype(BF), grad[:, lanes], ((0,), (0,)))
        for i, r in enumerate(rs):
            acc[r] += part[64 * i : 64 * i + 64]

    def two_heads(i, carry):
        one_head(2 * i)
        one_head(2 * i + 1)
        return carry

    lax.fori_loop(0, HEADS // 2, two_heads, 0)

    @pl.when(cube == pl.num_programs(0) - 1)
    def _():
        flush(acc, own, far, pairs, slots)


def fine_probs(rows, query, grad, keys, far_keys, slots, scale):
    cubes = query.shape[0] // 64
    pairs = cubes * HEADS
    devices = far_keys.shape[0]
    far_shape = (devices, slots * 64 + TRAILER, HEAD_DIM)
    width = HEADS * HEAD_DIM
    cube_block = pl.BlockSpec((64, width), lambda c, *_: (c, 0))
    return pl.pallas_call(
        functools.partial(probs_body, scale=scale, pairs=pairs, slots=slots),
        grid_spec=pltpu.PrefetchScalarGridSpec(
            num_scalar_prefetch=1,
            grid=(cubes,),
            in_specs=[cube_block, cube_block, whole(keys.shape), whole(far_keys.shape)],
            out_specs=[
                pl.BlockSpec((HEADS, 64, 512), lambda c, *_: (c, 0, 0)),
                whole((pairs, 64, HEAD_DIM)),
                whole(far_shape),
            ],
            scratch_shapes=[
                pltpu.VMEM((pairs + devices * slots, 64, HEAD_DIM), BF),
                pltpu.VMEM((pairs + devices * slots, 64, HEAD_DIM), F32),
            ],
        ),
        out_shape=[
            jax.ShapeDtypeStruct((pairs, 64, 512), F32),
            jax.ShapeDtypeStruct((pairs, 64, HEAD_DIM), F32),
            jax.ShapeDtypeStruct(far_shape, BF),
        ],
        compiler_params=VMEM,
        name="fine_probs",
    )(rows, query, grad, keys, far_keys)


def grads_body(
    rows, query, grad, keys, far_keys, values, far_values, weights,
    fine_out, fine_query, own, far, key_table, value_table, acc, *, scale, pairs, slots,
):
    cube = pl.program_id(0)

    @pl.when(cube == 0)
    def _():
        fill_table(key_table, keys, far_keys, pairs, slots)
        fill_table(value_table, values, far_values, pairs, slots)
        clear(acc)

    def one_head(h):
        lanes = head_lanes(h)
        rs = picked(rows, cube, h)
        key_rows = jnp.concatenate([key_table[r] for r in rs], axis=0)
        value_rows = jnp.concatenate([value_table[r] for r in rs], axis=0)
        g = grad[:, lanes]
        w = weights[h]
        out = mm(w.astype(BF), value_rows, ((1,), (0,)))
        delta = jnp.sum(g.astype(F32) * out, axis=1, keepdims=True)
        slope = mm(g, value_rows, ((1,), (1,)))
        ds = (w * (slope - delta)).astype(BF)
        fine_out[:, lanes] = out
        fine_query[:, lanes] = mm(ds, key_rows, ((1,), (0,))) * scale
        part = mm(ds, query[:, lanes], ((0,), (0,))) * scale
        for i, r in enumerate(rs):
            acc[r] += part[64 * i : 64 * i + 64]

    def two_heads(i, carry):
        one_head(2 * i)
        one_head(2 * i + 1)
        return carry

    lax.fori_loop(0, HEADS // 2, two_heads, 0)

    @pl.when(cube == pl.num_programs(0) - 1)
    def _():
        flush(acc, own, far, pairs, slots)


def fine_grads(rows, query, grad, keys, far_keys, values, far_values, weights, slots, scale):
    cubes = query.shape[0] // 64
    pairs = cubes * HEADS
    devices = far_keys.shape[0]
    far_shape = (devices, slots * 64, HEAD_DIM)
    width = HEADS * HEAD_DIM
    cube_block = pl.BlockSpec((64, width), lambda c, *_: (c, 0))
    table = (pairs + devices * slots, 64, HEAD_DIM)
    return pl.pallas_call(
        functools.partial(grads_body, scale=scale, pairs=pairs, slots=slots),
        grid_spec=pltpu.PrefetchScalarGridSpec(
            num_scalar_prefetch=1,
            grid=(cubes,),
            in_specs=[
                cube_block,
                cube_block,
                whole(keys.shape),
                whole(far_keys.shape),
                whole(values.shape),
                whole(far_values.shape),
                pl.BlockSpec((HEADS, 64, 512), lambda c, *_: (c, 0, 0)),
            ],
            out_specs=[
                cube_block,
                cube_block,
                whole((pairs, 64, HEAD_DIM)),
                whole(far_shape),
            ],
            scratch_shapes=[
                pltpu.VMEM(table, BF),
                pltpu.VMEM(table, BF),
                pltpu.VMEM(table, F32),
            ],
        ),
        out_shape=[
            jax.ShapeDtypeStruct(query.shape, F32),
            jax.ShapeDtypeStruct(query.shape, F32),
            jax.ShapeDtypeStruct((pairs, 64, HEAD_DIM), F32),
            jax.ShapeDtypeStruct(far_shape, BF),
        ],
        compiler_params=VMEM,
        name="fine_grads",
    )(rows, query, grad, keys, far_keys, values, far_values, weights)


def add_returned(pairs, own, back, trailer, acc, quantity):
    slots = pairs.shape[0] // back.shape[0]
    for p in range(own.shape[0]):
        c, h = p // HEADS, p % HEADS
        high = trailer[p, quantity : quantity + 1].astype(F32)
        low = trailer[p, TRAILER // 2 + quantity : TRAILER // 2 + quantity + 1].astype(F32)
        acc[cube_rows(c), head_lanes(h)] = own[p] + (high + low) * (1.0 / 64.0)

    def one(d, carry):
        for s in range(slots):
            p = pairs[d * slots + s]
            rows = cube_rows(p // HEADS)
            lanes = head_lanes(p % HEADS)
            acc[rows, lanes] += back[d, cube_rows(s)].astype(F32)
        return carry

    lax.fori_loop(0, back.shape[0], one, 0)


def collect_keys_body(pairs, own, back, trailer, out, acc):
    add_returned(pairs, own, back, trailer, acc, 2)
    out[...] = acc[...].astype(out.dtype)


PIECES = (
    (256, (0, 1, 0)),
    (16, (0, 0, 1)),
    (8, (0, 1, 1)),
    (128, (1, 0, 0)),
    (64, (1, 1, 0)),
    (8, (1, 0, 1)),
    (8, (1, 1, 1)),
    (128, (-1, 0, 0)),
    (64, (-1, 1, 0)),
    (8, (-1, 0, 1)),
    (8, (-1, 1, 1)),
)


def collect_values_body(pairs, half, own, back, trailer, out, *rest):
    pieces, acc = rest[:-1], rest[-1]
    add_returned(pairs, own, back, trailer, acc, 3)

    def lane_block(h, carry):
        lanes = head_lanes(h)
        for g in range(acc.shape[0] // 64):
            for i in range(16):
                row = 64 * g + 4 * i
                out[i // 4, i % 4, 4 * g : 4 * g + 4, lanes] = acc[row : row + 4, lanes]
        near, edge, near_edge = pieces[:3]
        for i in range(8):
            near[32 * i : 32 * i + 32, lanes] = out[i // 4, i % 4, :, lanes].astype(BF)
        column = jnp.concatenate(
            [
                jnp.where(
                    half[0] == 0,
                    out[i // 4, i % 4, 31:32, lanes],
                    out[i // 4, i % 4, 0:1, lanes],
                )
                for i in range(16)
            ],
            axis=0,
        )
        edge[:, lanes] = column.astype(BF)
        near_edge[:, lanes] = column[0:8].astype(BF)
        blank = jnp.zeros((1, HEAD_DIM), F32)
        for y, (row, near_row, corner, near_corner) in ((3, pieces[3:7]), (0, pieces[7:11])):
            for t in range(4):
                cells = out[t, y, :, lanes].astype(BF)
                row[32 * t : 32 * t + 32, lanes] = cells
                if t < 2:
                    near_row[32 * t : 32 * t + 32, lanes] = cells
            picks = [column[4 * t + y : 4 * t + y + 1] for t in range(4)]
            corner[:, lanes] = jnp.concatenate(picks + [blank] * 4, axis=0).astype(BF)
            near_corner[:, lanes] = jnp.concatenate(picks[:2] + [blank] * 6, axis=0).astype(BF)
        return carry

    lax.fori_loop(0, HEADS, lane_block, 0)


def collect(pairs, own, back, halves, half=None):
    cubes = own.shape[0] // HEADS
    width = HEADS * HEAD_DIM
    tokens = (cubes * 64, width)
    last = halves.shape[1] // TRAILER - 1
    if half is None:
        scalars, body = (pairs,), collect_keys_body
        shapes = [jax.ShapeDtypeStruct(tokens, BF)]
    else:
        scalars, body = (pairs, half), collect_values_body
        shapes = [jax.ShapeDtypeStruct((4, 4, 4 * cubes, width), F32)]
        shapes += [jax.ShapeDtypeStruct((rows, width), BF) for rows, _ in PIECES]
    return pl.pallas_call(
        body,
        grid_spec=pltpu.PrefetchScalarGridSpec(
            num_scalar_prefetch=len(scalars),
            grid=(1,),
            in_specs=[
                whole(own.shape),
                whole(back.shape),
                pl.BlockSpec((halves.shape[0], TRAILER, HEAD_DIM), lambda *_: (0, last, 0)),
            ],
            out_specs=[whole(x.shape) for x in shapes],
            scratch_shapes=[pltpu.VMEM(tokens, F32)],
        ),
        out_shape=shapes,
        compiler_params=VMEM,
        name="collect",
    )(*scalars, own, back, halves)


def put_tokens(out, sums, tokens):
    for i in range(16):
        for g in range(tokens.shape[0] // 64):
            row = 64 * g + 4 * i
            tokens[row : row + 4] = sums[i, 4 * g : 4 * g + 4]
    out[...] = tokens[...].astype(out.dtype)


def forward_body(framed, taps, out, wide, left, middle, right, sums, tokens):
    for p in range(36):
        wide[p, 0:34] = framed[p // 6, p % 6].astype(F32)
        left[p] = wide[p, 0:32]
        middle[p] = wide[p, 1:33]
        right[p] = wide[p, 2:34]

    def one(i, carry):
        f, y = i // 4, i % 4
        total = jnp.zeros((32, HEAD_DIM), F32)
        for back in range(3):
            for row in (-1, 0, 1):
                plane = (f + 2 - back) * 6 + y + 1 + row
                for col, cells in ((-1, left), (0, middle), (1, right)):
                    tap = 9 * back + 3 * (row + 1) + col + 1
                    total = total + taps[tap : tap + 1] * cells[plane]
        sums[i] = total
        return carry

    lax.fori_loop(0, 16, one, 0)
    put_tokens(out, sums, tokens)


def filter_forward(framed, taps):
    planes = framed.shape[0] * framed.shape[1]
    breadth, width = framed.shape[2] - 2, framed.shape[3]
    rows = 16 * breadth
    return pl.pallas_call(
        forward_body,
        grid=(HEADS,),
        in_specs=[
            pl.BlockSpec(framed.shape[:3] + (HEAD_DIM,), lambda i: (0, 0, 0, i)),
            pl.BlockSpec((taps.shape[0], HEAD_DIM), lambda i: (0, i)),
        ],
        out_specs=pl.BlockSpec((rows, HEAD_DIM), lambda i: (0, i)),
        scratch_shapes=[pltpu.VMEM((planes, 40, HEAD_DIM), F32)]
        + [pltpu.VMEM((planes, breadth, HEAD_DIM), F32)] * 3
        + [pltpu.VMEM((16, breadth, HEAD_DIM), F32), pltpu.VMEM((rows, HEAD_DIM), F32)],
        out_shape=jax.ShapeDtypeStruct((rows, width), BF),
        compiler_params=VMEM,
        name="filter_forward",
    )(framed, taps)


def back_body(flags, grad, *rest):
    pieces = rest[: len(PIECES)]
    taps, out, wide, left, middle, right, sums, tokens = rest[len(PIECES) :]
    near, edge, near_edge = pieces[:3]
    half = flags[0]
    small = [pieces[i][...].astype(F32) for i in (1, 2, 5, 6, 9, 10)]
    edge, near_edge, top_edge, near_top_edge, low_edge, near_low_edge = small
    blank = jnp.zeros((1, HEAD_DIM), F32)
    for t in range(6):
        for r in range(6):
            p = 6 * t + r
            n = t - 4
            shown = None
            if 1 <= r <= 4:
                if t < 4:
                    cells, k, source = grad[t, r - 1], 4 * t + r - 1, edge
                else:
                    i = 4 * n + r - 1
                    cells, k, source = near[32 * i : 32 * i + 32].astype(F32), i, near_edge
                    shown = flags[1] > 0
            else:
                row, near_row = pieces[3:5] if r == 0 else pieces[7:9]
                shown = flags[2 if r == 0 else 3] > 0
                if t < 4:
                    cells, k = row[32 * t : 32 * t + 32].astype(F32), t
                    source = top_edge if r == 0 else low_edge
                else:
                    cells, k = near_row[32 * n : 32 * n + 32].astype(F32), n
                    source = near_top_edge if r == 0 else near_low_edge
                    shown = shown & (flags[1] > 0)
            side = source[k : k + 1]
            if shown is not None:
                cells = jnp.where(shown, cells, 0.0)
                side = jnp.where(shown, side, 0.0)
            wide[p, 8:40] = cells
            wide[p, 7:8] = jnp.where(half == 1, side, blank)
            wide[p, 40:41] = jnp.where(half == 0, side, blank)
            left[p] = wide[p, 7:39]
            middle[p] = cells
            right[p] = wide[p, 9:41]

    def one(i, carry):
        f, y = i // 4, i % 4
        total = jnp.zeros((32, HEAD_DIM), F32)
        for back in range(3):
            for row in (-1, 0, 1):
                plane = (f + back) * 6 + y + 1 - row
                for col, cells in ((-1, right), (0, middle), (1, left)):
                    tap = 9 * back + 3 * (row + 1) + col + 1
                    total = total + taps[tap : tap + 1] * cells[plane]
        sums[i] = total
        return carry

    lax.fori_loop(0, 16, one, 0)
    put_tokens(out, sums, tokens)


def filter_back(flags, grad, pieces, taps):
    frames, height, breadth, width = grad.shape
    rows = frames * height * breadth
    planes = (frames + 2) * (height + 2)
    return pl.pallas_call(
        back_body,
        grid_spec=pltpu.PrefetchScalarGridSpec(
            num_scalar_prefetch=1,
            grid=(HEADS,),
            in_specs=[pl.BlockSpec(grad.shape[:3] + (HEAD_DIM,), lambda i, *_: (0, 0, 0, i))]
            + [pl.BlockSpec((x.shape[0], HEAD_DIM), lambda i, *_: (0, i)) for x in (*pieces, taps)],
            out_specs=pl.BlockSpec((rows, HEAD_DIM), lambda i, *_: (0, i)),
            scratch_shapes=[pltpu.VMEM((planes, 48, HEAD_DIM), F32)]
            + [pltpu.VMEM((planes, breadth, HEAD_DIM), F32)] * 3
            + [
                pltpu.VMEM((frames * height, breadth, HEAD_DIM), F32),
                pltpu.VMEM((rows, HEAD_DIM), F32),
            ],
        ),
        out_shape=jax.ShapeDtypeStruct((rows, width), BF),
        compiler_params=VMEM,
        name="filter_back",
    )(flags, grad, *pieces, taps)


def put_halves(target, sem, stage, parts):
    for i, part in enumerate(parts):
        high = part.astype(BF)
        stage[:, i] = high
        stage[:, len(parts) + i] = (part - high.astype(F32)).astype(BF)
    rows = target.shape[1]
    copy = pltpu.make_async_copy(
        stage, target.at[:, pl.ds(rows - TRAILER, TRAILER)], sem
    )
    copy.start()
    copy.wait()


def from_halves(received):
    halves = received[:, -TRAILER:].astype(F32)
    return halves[:, : TRAILER // 2] + halves[:, TRAILER // 2 :]


def coarse_body(block, query, key, grad, value, back, out, stage, sem, *, scale):
    del back
    q, k, g, v = query[...], key[...], grad[...], value[...]
    logits = mm(k, q, ((1,), (1,))) * scale
    expo = jnp.exp(logits - jnp.max(logits, axis=0, keepdims=True))
    w = expo / jnp.sum(expo, axis=0, keepdims=True)
    wr = w.astype(BF)
    slope = mm(v, g, ((1,), (1,)))
    delta = jnp.sum(wr.astype(F32) * slope, axis=0, keepdims=True)
    ds = (w * (slope - delta)).astype(BF)
    results = (
        mm(wr, v, ((0,), (0,))),
        mm(ds, k, ((0,), (0,))) * scale,
        mm(ds, q, ((1,), (0,))) * scale,
        mm(wr, g, ((1,), (0,))),
    )
    shape = (results[0].shape[0] // 8, 8, HEAD_DIM)
    mine = lax.broadcasted_iota(jnp.int32, shape, 1) == block[0]
    parts = [jnp.sum(jnp.where(mine, r.reshape(shape), 0.0), axis=1) for r in results]
    put_halves(out, sem, stage, parts)


def coarse_head(block, pooled, back, scale):
    anywhere = pl.BlockSpec(memory_space=pl.ANY)
    return pl.pallas_call(
        functools.partial(coarse_body, scale=scale),
        grid_spec=pltpu.PrefetchScalarGridSpec(
            num_scalar_prefetch=1,
            grid=(1,),
            in_specs=[whole(x.shape) for x in pooled] + [anywhere],
            out_specs=anywhere,
            scratch_shapes=[
                pltpu.VMEM((back.shape[0], TRAILER, HEAD_DIM), BF),
                pltpu.SemaphoreType.DMA,
            ],
        ),
        out_shape=jax.ShapeDtypeStruct(back.shape, back.dtype),
        input_output_aliases={5: 0},
        compiler_params=VMEM,
        name="coarse_head",
    )(block, *pooled, back)


def taps_body(member, grad, framed, out, wide):
    del member
    frames, height, breadth = grad.shape[:3]
    planes, rows = framed.shape[:2]
    for t in range(planes):
        for r in range(rows):
            wide[t * rows + r, 0 : framed.shape[2]] = framed[t, r].astype(F32)
    for col in range(3):
        sums = {}
        for t in range(planes):
            for r in range(rows):
                cells = wide[t * rows + r, col : col + breadth]
                for back in range(3):
                    for row in range(3):
                        f, y = t - 2 + back, r - row
                        if 0 <= f < frames and 0 <= y < height:
                            tap = 9 * back + 3 * row + col
                            term = jnp.sum((grad[f, y] * cells).reshape(-1, 8, 128), axis=0)
                            sums[tap] = sums[tap] + term if tap in sums else term
        for tap, total in sums.items():
            out[0, tap : tap + 1] = jnp.sum(total, axis=0, keepdims=True)
    out[0, 27:] = jnp.zeros((5, 128), F32)


def tap_gradients(member, grad, framed):
    return pl.pallas_call(
        taps_body,
        grid_spec=pltpu.PrefetchScalarGridSpec(
            num_scalar_prefetch=1,
            grid=(HEADS,),
            in_specs=[
                pl.BlockSpec(grad.shape[:3] + (128,), lambda i, m: (0, 0, 0, i)),
                pl.BlockSpec(framed.shape[:3] + (128,), lambda i, m: (0, 0, 0, i)),
            ],
            out_specs=pl.BlockSpec(
                (1, 32, 128), lambda i, m: ((i + HEADS - m[0]) % HEADS, 0, 0)
            ),
            scratch_shapes=[pltpu.VMEM((framed.shape[0] * framed.shape[1], 40, 128), F32)],
        ),
        out_shape=jax.ShapeDtypeStruct((HEADS, 32, 128), F32),
        compiler_params=VMEM,
        name="tap_gradients",
    )(member, grad, framed)


def shifted(block, steps):
    count = lax.axis_size("seq")
    return lax.ppermute(block, "seq", [(i, (i + steps) % count) for i in range(count)])


def with_neighbours(lattice, forward, place, ready, held):
    row_band, slab_index, col_half, band_count = place
    half = lax.axis_size("seq") // 2
    own = lattice.astype(BF)
    edge = jnp.where(col_half == 0, own[:, :, -1:], own[:, :, :1])
    frames = slice(-2, None) if forward else slice(0, 2)
    steps = band_count if forward else -band_count
    has_slab = slab_index > 0 if forward else slab_index < SLABS - 1
    own_edge = shifted(edge, half)
    near = shifted(own[frames], steps)
    near_edge = shifted(edge[frames], steps + half)
    near = jnp.where(has_slab, near, jnp.zeros_like(near)).astype(lattice.dtype)
    near_edge = jnp.where(has_slab, near_edge, jnp.zeros_like(near_edge))
    order = (lambda a, b: [a, b]) if forward else (lambda a, b: [b, a])
    middle = jnp.concatenate(order(near, lattice), axis=0)
    edges = jnp.concatenate(order(near_edge, own_edge), axis=0).astype(lattice.dtype)
    wide = side_columns(middle, edges, col_half)
    top, bottom = wide[:, :1].astype(BF), wide[:, -1:].astype(BF)
    top, bottom = together(top, bottom, ready)[:2]
    above, below, held = together(shifted(bottom, 1), shifted(top, -1), held)
    above = jnp.where(row_band > 0, above, jnp.zeros_like(above)).astype(lattice.dtype)
    below = jnp.where(row_band < band_count - 1, below, jnp.zeros_like(below))
    return jnp.concatenate([above, wide, below.astype(lattice.dtype)], axis=1), held


def to_lattice(tokens):
    channels = tokens.shape[1]
    cube_count = tokens.shape[0] // 64
    lattice = tokens.reshape(cube_count, 4, 4, 4, channels).transpose(1, 2, 0, 3, 4)
    return lattice.reshape(4, 4, cube_count * 4, channels)


def side_columns(lattice, edge, col_half):
    blank = jnp.zeros_like(edge)
    return jnp.concatenate(
        [jnp.where(col_half == 1, edge, blank), lattice, jnp.where(col_half == 0, edge, blank)],
        axis=2,
    )


def pool_cubes(tokens):
    return jnp.mean(
        tokens.astype(jnp.float32).reshape(tokens.shape[0] // 64, 64, tokens.shape[1]), axis=1
    )


def spread(per_cube):
    cube_count = per_cube.shape[0]
    return jnp.broadcast_to(per_cube[:, None, :], (cube_count, 64, per_cube.shape[1])).reshape(
        cube_count * 64, per_cube.shape[1]
    )


def exchanged(rows, groups=None):
    return lax.all_to_all(
        rows, "seq", split_axis=0, concat_axis=0, tiled=True, axis_index_groups=groups
    )


def in_plane(block, ahead):
    count = lax.axis_size("seq")
    return lax.ppermute(
        block, "seq", [(i, i // HEADS * HEADS + (i + ahead) % HEADS) for i in range(count)]
    )


def together(*values):
    return lax.optimization_barrier(values)


def shards(query_tokens, key_tokens, value_tokens, gate_tokens, filter_taps, selected, cotangent):
    devices = lax.axis_size("seq")
    device_index = lax.axis_index("seq")
    cube_count = query_tokens.shape[0] // 64
    pair_count = cube_count * HEADS
    channels = HEADS * HEAD_DIM
    capacity = max(3, 2 * HEADS * POOL // (devices - 1))
    logit_scale = HEAD_DIM ** (-0.5)
    band_count = devices // (2 * SLABS)
    rotated = (device_index + 2 * band_count + band_count // 2) % devices
    row_band = rotated % band_count
    slab_index = rotated // band_count % SLABS
    col_half = rotated // (devices // 2)

    owner_device = selected // cube_count
    pair_index = selected % cube_count * HEADS + jnp.arange(HEADS, dtype=jnp.int32)[None, :, None]
    owner_flat, pair_flat = owner_device.reshape(-1), pair_index.reshape(-1)
    remote_flat = owner_flat != device_index
    of_owner = (owner_flat[:, None] == jnp.arange(devices, dtype=jnp.int32)) & remote_flat[:, None]
    of_owner = of_owner.astype(BF)
    pair_ids = jnp.arange(pair_count, dtype=jnp.int32)
    of_pair = (pair_flat[:, None] == pair_ids).astype(BF)
    present = mm(of_owner, of_pair, ((0,), (0,))) > 0.5
    earlier = (pair_ids[:, None] < pair_ids).astype(BF)
    slot_rank = mm(present.astype(BF), earlier, ((1,), (0,)))
    in_slot = (slot_rank[:, None, :] == jnp.arange(capacity, dtype=F32)[None, :, None]) & (
        present[:, None, :]
    )
    requests = jnp.sum(jnp.where(in_slot, pair_ids, 0), axis=2).reshape(-1)
    asked_pairs = exchanged(requests)
    owner_rank = mm(of_owner, slot_rank.astype(BF), ((1,), (0,)))
    slot_of = jnp.sum(owner_rank * of_pair.astype(F32), axis=1).astype(jnp.int32)
    table_row = jnp.where(
        remote_flat, pair_count + owner_flat * capacity + slot_of, pair_flat
    )

    place = (row_band, slab_index, col_half, band_count)
    framed, asked_keys = with_neighbours(
        to_lattice(value_tokens), True, place, asked_pairs,
        gather_pairs(asked_pairs, key_tokens, devices),
    )
    far_keys = exchanged(asked_keys)

    filtered = filter_forward(framed, filter_taps)
    gated = cotangent.astype(F32) * gate_tokens.astype(F32)
    pooled = jnp.stack(
        [
            pool_cubes(query_tokens).astype(BF),
            pool_cubes(key_tokens).astype(BF),
            jnp.sum(gated.reshape(cube_count, 64, channels), axis=1).astype(BF),
            pool_cubes(filtered).astype(BF),
        ],
        axis=1,
    )
    pooled = pooled.reshape(cube_count, 4, HEADS, HEAD_DIM).transpose(2, 1, 0, 3)
    pooled = pooled.reshape(HEADS, 4 * cube_count, HEAD_DIM)
    far_values = exchanged(gather_pairs(asked_pairs, filtered, devices, pooled))
    one_head = far_values[:, capacity * 64 :].reshape(devices, 4, cube_count, HEAD_DIM)
    one_head = one_head.transpose(1, 0, 2, 3).reshape(4, devices * cube_count, HEAD_DIM)

    weights, own_value, back_value = fine_probs(
        table_row, query_tokens, cotangent, key_tokens, far_keys, capacity, logit_scale
    )
    block = (device_index // HEADS).reshape(1)
    back_value = exchanged(coarse_head(block, tuple(one_head), back_value, logit_scale))
    fine_out, fine_query, own_key, back_key = fine_grads(
        table_row, query_tokens, cotangent, key_tokens, far_keys, filtered, far_values, weights,
        capacity, logit_scale,
    )
    coarse = from_halves(back_value).reshape(cube_count, HEADS, 4, HEAD_DIM)
    coarse = coarse.transpose(2, 0, 1, 3).reshape(4, cube_count, channels)
    coarse_out, coarse_query = coarse[:2]

    coarse_tokens = spread(coarse_out)
    attended = (fine_out + gate_tokens.astype(F32) * coarse_tokens).astype(BF)
    gate_gradient = (cotangent.astype(F32) * coarse_tokens).astype(BF)
    query_gradient = (fine_query + spread(coarse_query) / 64.0).astype(BF)

    back_key, back_value = together(back_key, back_value)
    back_key = exchanged(back_key)
    grad_lattice, *pieces = collect(
        asked_pairs, own_value, back_value, back_value, col_half.reshape(1)
    )
    cells = [
        shifted(piece, rows - band_count * slabs + devices // 2 * halves)
        for piece, (_, (rows, slabs, halves)) in zip(pieces, PIECES)
    ]
    shares = tap_gradients((device_index % HEADS).reshape(1), grad_lattice, framed)
    mates = [in_plane(shares[ahead], ahead) for ahead in range(1, HEADS)]

    back_key, attended, query_gradient, gate_gradient, *arrived = together(
        back_key, attended, query_gradient, gate_gradient, *cells, *mates
    )
    cells, mates = arrived[: len(cells)], arrived[len(cells) :]
    taps = sum(mates, shares[0])
    rest = devices // HEADS
    columns = [[HEADS * b + h for b in range(rest)] for h in range(HEADS)]
    planes = [[HEADS * b + h for h in range(HEADS)] for b in range(rest)]
    taps = exchanged(jnp.broadcast_to(taps[None], (rest, 32, 128)), columns)
    (key_gradient,) = collect(asked_pairs, own_key, back_key, back_value)
    taps, key_gradient = together(taps, key_gradient)
    taps = jnp.sum(taps, axis=0)
    taps = exchanged(jnp.broadcast_to(taps[None], (HEADS, 32, 128)), planes)
    filter_gradient = taps.transpose(1, 0, 2).reshape(32, channels)[: filter_taps.shape[0]]
    flags = jnp.stack(
        [
            col_half,
            (slab_index < SLABS - 1).astype(jnp.int32),
            (row_band > 0).astype(jnp.int32),
            (row_band < band_count - 1).astype(jnp.int32),
        ]
    )
    value_gradient = filter_back(flags, grad_lattice, cells, filter_taps)
    return (attended, query_gradient, key_gradient, value_gradient, gate_gradient, filter_gradient)


def solution(mesh):
    return jax.shard_map(
        shards,
        mesh=mesh,
        in_specs=(
            P(("dp", "seq"), None),
            P(("dp", "seq"), None),
            P(("dp", "seq"), None),
            P(("dp", "seq"), None),
            P(),
            P(("dp", "seq"), None, None),
            P(("dp", "seq"), None),
        ),
        out_specs=(
            P(("dp", "seq"), None),
            P(("dp", "seq"), None),
            P(("dp", "seq"), None),
            P(("dp", "seq"), None),
            P(("dp", "seq"), None),
            P("dp", None),
        ),
        check_vma=False,
    )
```

```python
import functools
import jax
import jax.numpy as jnp
from jax import lax
from jax.experimental import pallas as pl
from jax.experimental.pallas import tpu as pltpu
from jax.sharding import PartitionSpec as P

HEAD_DIM = 128
HEADS = 8
SLABS = 4
POOL = 12
BF = jnp.bfloat16
F32 = jnp.float32
TRAILER = 8
VMEM = pltpu.CompilerParams(vmem_limit_bytes=56 << 20)


def head_lanes(h):
    if isinstance(h, int):
        return slice(h * HEAD_DIM, (h + 1) * HEAD_DIM)
    return pl.ds(pl.multiple_of(h * HEAD_DIM, HEAD_DIM), HEAD_DIM)


def cube_rows(c):
    if isinstance(c, int):
        return slice(c * 64, c * 64 + 64)
    return pl.ds(pl.multiple_of(c * 64, 64), 64)


def mm(a, b, dims):
    return lax.dot_general(a, b, (dims, ((), ())), preferred_element_type=F32)


def whole(shape):
    zeros = (0,) * len(shape)
    return pl.BlockSpec(shape, lambda *_: zeros)


def gather_body(pairs, tokens, *rest, dests, slots):
    extra, out = rest if len(rest) == 2 else (None, rest[0])
    base = pl.program_id(0) * dests

    def one(d, carry):
        for s in range(slots):
            p = pairs[(base + d) * slots + s]
            out[d, cube_rows(s)] = tokens[cube_rows(p // HEADS), head_lanes(p % HEADS)]
        if extra is not None:
            out[d, slots * 64 :] = extra[d % HEADS]
        return carry

    lax.fori_loop(0, dests, one, 0)


def gather_pairs(pairs, tokens, devices, extra=None):
    slots = pairs.shape[0] // devices
    dests = devices // 4
    rows = slots * 64 + (0 if extra is None else extra.shape[1])
    operands = (tokens,) if extra is None else (tokens, extra)
    return pl.pallas_call(
        functools.partial(gather_body, dests=dests, slots=slots),
        grid_spec=pltpu.PrefetchScalarGridSpec(
            num_scalar_prefetch=1,
            grid=(4,),
            in_specs=[whole(x.shape) for x in operands],
            out_specs=pl.BlockSpec((dests, rows, HEAD_DIM), lambda i, *_: (i, 0, 0)),
        ),
        out_shape=jax.ShapeDtypeStruct((devices, rows, HEAD_DIM), tokens.dtype),
        compiler_params=VMEM,
        name="gather_pairs",
    )(pairs, *operands)


def fill_table(table, tokens, fetched, pairs, slots):
    def near(p, carry):
        table[p] = tokens[cube_rows(p // HEADS), head_lanes(p % HEADS)]
        return carry

    lax.fori_loop(0, pairs, near, 0)

    def one(d, carry):
        for s in range(slots):
            table[pairs + d * slots + s] = fetched[d, cube_rows(s)]
        return carry

    lax.fori_loop(0, fetched.shape[0], one, 0)


def clear(acc):
    def one(i, carry):
        acc[i] = jnp.zeros(acc.shape[1:], acc.dtype)
        return carry

    lax.fori_loop(0, acc.shape[0], one, 0, unroll=2)


def flush(acc, own, far, pairs, slots):
    def near(i, carry):
        own[i] = acc[i]
        return carry

    def distant(d, carry):
        for s in range(slots):
            far[d, cube_rows(s)] = acc[pairs + d * slots + s].astype(far.dtype)
        if far.shape[1] > slots * 64:
            far[d, slots * 64 :] = jnp.zeros((TRAILER, HEAD_DIM), far.dtype)
        return carry

    lax.fori_loop(0, pairs, near, 0)
    lax.fori_loop(0, far.shape[0], distant, 0)


def picked(rows, cube, h):
    return [rows[(cube * HEADS + h) * 8 + i] for i in range(8)]


def probs_body(rows, query, grad, keys, far_keys, weights, own, far, table, acc, *, scale, pairs, slots):
    cube = pl.program_id(0)

    @pl.when(cube == 0)
    def _():
        fill_table(table, keys, far_keys, pairs, slots)
        clear(acc)

    def one_head(h):
        lanes = head_lanes(h)
        rs = picked(rows, cube, h)
        key_rows = jnp.concatenate([table[r] for r in rs], axis=0)
        logits = mm(query[:, lanes], key_rows, ((1,), (1,))) * scale
        expo = jnp.exp(logits - jnp.max(logits, axis=1, keepdims=True))
        w = expo / jnp.sum(expo, axis=1, keepdims=True)
        weights[h] = w
        part = mm(w.astype(BF), grad[:, lanes], ((0,), (0,)))
        for i, r in enumerate(rs):
            acc[r] += part[64 * i : 64 * i + 64]

    def two_heads(i, carry):
        one_head(2 * i)
        one_head(2 * i + 1)
        return carry

    lax.fori_loop(0, HEADS // 2, two_heads, 0)

    @pl.when(cube == pl.num_programs(0) - 1)
    def _():
        flush(acc, own, far, pairs, slots)


def fine_probs(rows, query, grad, keys, far_keys, slots, scale):
    cubes = query.shape[0] // 64
    pairs = cubes * HEADS
    devices = far_keys.shape[0]
    far_shape = (devices, slots * 64 + TRAILER, HEAD_DIM)
    width = HEADS * HEAD_DIM
    cube_block = pl.BlockSpec((64, width), lambda c, *_: (c, 0))
    return pl.pallas_call(
        functools.partial(probs_body, scale=scale, pairs=pairs, slots=slots),
        grid_spec=pltpu.PrefetchScalarGridSpec(
            num_scalar_prefetch=1,
            grid=(cubes,),
            in_specs=[cube_block, cube_block, whole(keys.shape), whole(far_keys.shape)],
            out_specs=[
                pl.BlockSpec((HEADS, 64, 512), lambda c, *_: (c, 0, 0)),
                whole((pairs, 64, HEAD_DIM)),
                whole(far_shape),
            ],
            scratch_shapes=[
                pltpu.VMEM((pairs + devices * slots, 64, HEAD_DIM), BF),
                pltpu.VMEM((pairs + devices * slots, 64, HEAD_DIM), F32),
            ],
        ),
        out_shape=[
            jax.ShapeDtypeStruct((pairs, 64, 512), F32),
            jax.ShapeDtypeStruct((pairs, 64, HEAD_DIM), F32),
            jax.ShapeDtypeStruct(far_shape, BF),
        ],
        compiler_params=VMEM,
        name="fine_probs",
    )(rows, query, grad, keys, far_keys)


def grads_body(
    rows, query, grad, keys, far_keys, values, far_values, weights,
    fine_out, fine_query, own, far, key_table, value_table, acc, *, scale, pairs, slots,
):
    cube = pl.program_id(0)

    @pl.when(cube == 0)
    def _():
        fill_table(key_table, keys, far_keys, pairs, slots)
        fill_table(value_table, values, far_values, pairs, slots)
        clear(acc)

    def one_head(h):
        lanes = head_lanes(h)
        rs = picked(rows, cube, h)
        key_rows = jnp.concatenate([key_table[r] for r in rs], axis=0)
        value_rows = jnp.concatenate([value_table[r] for r in rs], axis=0)
        g = grad[:, lanes]
        w = weights[h]
        out = mm(w.astype(BF), value_rows, ((1,), (0,)))
        delta = jnp.sum(g.astype(F32) * out, axis=1, keepdims=True)
        slope = mm(g, value_rows, ((1,), (1,)))
        ds = (w * (slope - delta)).astype(BF)
        fine_out[:, lanes] = out
        fine_query[:, lanes] = mm(ds, key_rows, ((1,), (0,))) * scale
        part = mm(ds, query[:, lanes], ((0,), (0,))) * scale
        for i, r in enumerate(rs):
            acc[r] += part[64 * i : 64 * i + 64]

    def two_heads(i, carry):
        one_head(2 * i)
        one_head(2 * i + 1)
        return carry

    lax.fori_loop(0, HEADS // 2, two_heads, 0)

    @pl.when(cube == pl.num_programs(0) - 1)
    def _():
        flush(acc, own, far, pairs, slots)


def fine_grads(rows, query, grad, keys, far_keys, values, far_values, weights, slots, scale):
    cubes = query.shape[0] // 64
    pairs = cubes * HEADS
    devices = far_keys.shape[0]
    far_shape = (devices, slots * 64, HEAD_DIM)
    width = HEADS * HEAD_DIM
    cube_block = pl.BlockSpec((64, width), lambda c, *_: (c, 0))
    table = (pairs + devices * slots, 64, HEAD_DIM)
    return pl.pallas_call(
        functools.partial(grads_body, scale=scale, pairs=pairs, slots=slots),
        grid_spec=pltpu.PrefetchScalarGridSpec(
            num_scalar_prefetch=1,
            grid=(cubes,),
            in_specs=[
                cube_block,
                cube_block,
                whole(keys.shape),
                whole(far_keys.shape),
                whole(values.shape),
                whole(far_values.shape),
                pl.BlockSpec((HEADS, 64, 512), lambda c, *_: (c, 0, 0)),
            ],
            out_specs=[
                cube_block,
                cube_block,
                whole((pairs, 64, HEAD_DIM)),
                whole(far_shape),
            ],
            scratch_shapes=[
                pltpu.VMEM(table, BF),
                pltpu.VMEM(table, BF),
                pltpu.VMEM(table, F32),
            ],
        ),
        out_shape=[
            jax.ShapeDtypeStruct(query.shape, F32),
            jax.ShapeDtypeStruct(query.shape, F32),
            jax.ShapeDtypeStruct((pairs, 64, HEAD_DIM), F32),
            jax.ShapeDtypeStruct(far_shape, BF),
        ],
        compiler_params=VMEM,
        name="fine_grads",
    )(rows, query, grad, keys, far_keys, values, far_values, weights)


def add_returned(pairs, own, back, trailer, acc, quantity):
    step, steps = pl.program_id(0), pl.num_programs(0)
    owners = back.shape[0]
    slots = pairs.shape[0] // (owners * steps)

    @pl.when(step == 0)
    def _():
        for p in range(own.shape[0]):
            c, h = p // HEADS, p % HEADS
            high = trailer[p, quantity : quantity + 1].astype(F32)
            low = trailer[p, TRAILER // 2 + quantity : TRAILER // 2 + quantity + 1].astype(F32)
            acc[cube_rows(c), head_lanes(h)] = own[p] + (high + low) * (1.0 / 64.0)

    def one(d, carry):
        for s in range(slots):
            p = pairs[(step * owners + d) * slots + s]
            rows = cube_rows(p // HEADS)
            lanes = head_lanes(p % HEADS)
            acc[rows, lanes] += back[d, cube_rows(s)].astype(F32)
        return carry

    lax.fori_loop(0, owners, one, 0)


def collect_keys_body(pairs, own, back, trailer, out, acc):
    add_returned(pairs, own, back, trailer, acc, 2)

    @pl.when(pl.program_id(0) == pl.num_programs(0) - 1)
    def _():
        out[...] = acc[...].astype(out.dtype)


PIECES = (
    (256, (0, 1, 0)),
    (16, (0, 0, 1)),
    (8, (0, 1, 1)),
    (128, (1, 0, 0)),
    (64, (1, 1, 0)),
    (8, (1, 0, 1)),
    (8, (1, 1, 1)),
    (128, (-1, 0, 0)),
    (64, (-1, 1, 0)),
    (8, (-1, 0, 1)),
    (8, (-1, 1, 1)),
)


def collect_values_body(pairs, half, own, back, trailer, out, *rest):
    pieces, acc = rest[:-1], rest[-1]
    add_returned(pairs, own, back, trailer, acc, 3)

    def lane_block(h, carry):
        lanes = head_lanes(h)
        for g in range(acc.shape[0] // 64):
            for i in range(16):
                row = 64 * g + 4 * i
                out[i // 4, i % 4, 4 * g : 4 * g + 4, lanes] = acc[row : row + 4, lanes]
        near, edge, near_edge = pieces[:3]
        for i in range(8):
            near[32 * i : 32 * i + 32, lanes] = out[i // 4, i % 4, :, lanes].astype(BF)
        column = jnp.concatenate(
            [
                jnp.where(
                    half[0] == 0,
                    out[i // 4, i % 4, 31:32, lanes],
                    out[i // 4, i % 4, 0:1, lanes],
                )
                for i in range(16)
            ],
            axis=0,
        )
        edge[:, lanes] = column.astype(BF)
        near_edge[:, lanes] = column[0:8].astype(BF)
        blank = jnp.zeros((1, HEAD_DIM), F32)
        for y, (row, near_row, corner, near_corner) in ((3, pieces[3:7]), (0, pieces[7:11])):
            for t in range(4):
                cells = out[t, y, :, lanes].astype(BF)
                row[32 * t : 32 * t + 32, lanes] = cells
                if t < 2:
                    near_row[32 * t : 32 * t + 32, lanes] = cells
            picks = [column[4 * t + y : 4 * t + y + 1] for t in range(4)]
            corner[:, lanes] = jnp.concatenate(picks + [blank] * 4, axis=0).astype(BF)
            near_corner[:, lanes] = jnp.concatenate(picks[:2] + [blank] * 6, axis=0).astype(BF)
        return carry

    @pl.when(pl.program_id(0) == pl.num_programs(0) - 1)
    def _():
        lax.fori_loop(0, HEADS, lane_block, 0)


def collect(pairs, own, back, halves, half=None):
    cubes = own.shape[0] // HEADS
    width = HEADS * HEAD_DIM
    tokens = (cubes * 64, width)
    last = halves.shape[1] // TRAILER - 1
    if half is None:
        scalars, body = (pairs,), collect_keys_body
        shapes = [jax.ShapeDtypeStruct(tokens, BF)]
    else:
        scalars, body = (pairs, half), collect_values_body
        shapes = [jax.ShapeDtypeStruct((4, 4, 4 * cubes, width), F32)]
        shapes += [jax.ShapeDtypeStruct((rows, width), BF) for rows, _ in PIECES]
    return pl.pallas_call(
        body,
        grid_spec=pltpu.PrefetchScalarGridSpec(
            num_scalar_prefetch=len(scalars),
            grid=(4,),
            in_specs=[
                whole(own.shape),
                pl.BlockSpec((back.shape[0] // 4,) + back.shape[1:], lambda i, *_: (i, 0, 0)),
                pl.BlockSpec((halves.shape[0], TRAILER, HEAD_DIM), lambda *_: (0, last, 0)),
            ],
            out_specs=[whole(x.shape) for x in shapes],
            scratch_shapes=[pltpu.VMEM(tokens, F32)],
        ),
        out_shape=shapes,
        compiler_params=VMEM,
        name="collect",
    )(*scalars, own, back, halves)


def put_tokens(out, sums, tokens):
    for i in range(16):
        for g in range(tokens.shape[0] // 64):
            row = 64 * g + 4 * i
            tokens[row : row + 4] = sums[i, 4 * g : 4 * g + 4]
    out[...] = tokens[...].astype(out.dtype)


def forward_body(framed, taps, out, wide, left, middle, right, sums, tokens):
    for p in range(36):
        wide[p, 0:34] = framed[p // 6, p % 6].astype(F32)
        left[p] = wide[p, 0:32]
        middle[p] = wide[p, 1:33]
        right[p] = wide[p, 2:34]

    def one(i, carry):
        f, y = i // 4, i % 4
        total = jnp.zeros((32, HEAD_DIM), F32)
        for back in range(3):
            for row in (-1, 0, 1):
                plane = (f + 2 - back) * 6 + y + 1 + row
                for col, cells in ((-1, left), (0, middle), (1, right)):
                    tap = 9 * back + 3 * (row + 1) + col + 1
                    total = total + taps[tap : tap + 1] * cells[plane]
        sums[i] = total
        return carry

    lax.fori_loop(0, 16, one, 0)
    put_tokens(out, sums, tokens)


def filter_forward(framed, taps):
    planes = framed.shape[0] * framed.shape[1]
    breadth, width = framed.shape[2] - 2, framed.shape[3]
    rows = 16 * breadth
    return pl.pallas_call(
        forward_body,
        grid=(HEADS,),
        in_specs=[
            pl.BlockSpec(framed.shape[:3] + (HEAD_DIM,), lambda i: (0, 0, 0, i)),
            pl.BlockSpec((taps.shape[0], HEAD_DIM), lambda i: (0, i)),
        ],
        out_specs=pl.BlockSpec((rows, HEAD_DIM), lambda i: (0, i)),
        scratch_shapes=[pltpu.VMEM((planes, 40, HEAD_DIM), F32)]
        + [pltpu.VMEM((planes, breadth, HEAD_DIM), F32)] * 3
        + [pltpu.VMEM((16, breadth, HEAD_DIM), F32), pltpu.VMEM((rows, HEAD_DIM), F32)],
        out_shape=jax.ShapeDtypeStruct((rows, width), BF),
        compiler_params=VMEM,
        name="filter_forward",
    )(framed, taps)


def back_body(flags, grad, *rest):
    pieces = rest[: len(PIECES)]
    taps, out, wide, left, middle, right, sums, tokens = rest[len(PIECES) :]
    near, edge, near_edge = pieces[:3]
    half = flags[0]
    small = [pieces[i][...].astype(F32) for i in (1, 2, 5, 6, 9, 10)]
    edge, near_edge, top_edge, near_top_edge, low_edge, near_low_edge = small
    blank = jnp.zeros((1, HEAD_DIM), F32)
    for t in range(6):
        for r in range(6):
            p = 6 * t + r
            n = t - 4
            shown = None
            if 1 <= r <= 4:
                if t < 4:
                    cells, k, source = grad[t, r - 1], 4 * t + r - 1, edge
                else:
                    i = 4 * n + r - 1
                    cells, k, source = near[32 * i : 32 * i + 32].astype(F32), i, near_edge
                    shown = flags[1] > 0
            else:
                row, near_row = pieces[3:5] if r == 0 else pieces[7:9]
                shown = flags[2 if r == 0 else 3] > 0
                if t < 4:
                    cells, k = row[32 * t : 32 * t + 32].astype(F32), t
                    source = top_edge if r == 0 else low_edge
                else:
                    cells, k = near_row[32 * n : 32 * n + 32].astype(F32), n
                    source = near_top_edge if r == 0 else near_low_edge
                    shown = shown & (flags[1] > 0)
            side = source[k : k + 1]
            if shown is not None:
                cells = jnp.where(shown, cells, 0.0)
                side = jnp.where(shown, side, 0.0)
            wide[p, 8:40] = cells
            wide[p, 7:8] = jnp.where(half == 1, side, blank)
            wide[p, 40:41] = jnp.where(half == 0, side, blank)
            left[p] = wide[p, 7:39]
            middle[p] = cells
            right[p] = wide[p, 9:41]

    def one(i, carry):
        f, y = i // 4, i % 4
        total = jnp.zeros((32, HEAD_DIM), F32)
        for back in range(3):
            for row in (-1, 0, 1):
                plane = (f + back) * 6 + y + 1 - row
                for col, cells in ((-1, right), (0, middle), (1, left)):
                    tap = 9 * back + 3 * (row + 1) + col + 1
                    total = total + taps[tap : tap + 1] * cells[plane]
        sums[i] = total
        return carry

    lax.fori_loop(0, 16, one, 0, unroll=2)
    put_tokens(out, sums, tokens)


def filter_back(flags, grad, pieces, taps):
    frames, height, breadth, width = grad.shape
    rows = frames * height * breadth
    planes = (frames + 2) * (height + 2)
    return pl.pallas_call(
        back_body,
        grid_spec=pltpu.PrefetchScalarGridSpec(
            num_scalar_prefetch=1,
            grid=(HEADS,),
            in_specs=[pl.BlockSpec(grad.shape[:3] + (HEAD_DIM,), lambda i, *_: (0, 0, 0, i))]
            + [pl.BlockSpec((x.shape[0], HEAD_DIM), lambda i, *_: (0, i)) for x in (*pieces, taps)],
            out_specs=pl.BlockSpec((rows, HEAD_DIM), lambda i, *_: (0, i)),
            scratch_shapes=[pltpu.VMEM((planes, 48, HEAD_DIM), F32)]
            + [pltpu.VMEM((planes, breadth, HEAD_DIM), F32)] * 3
            + [
                pltpu.VMEM((frames * height, breadth, HEAD_DIM), F32),
                pltpu.VMEM((rows, HEAD_DIM), F32),
            ],
        ),
        out_shape=jax.ShapeDtypeStruct((rows, width), BF),
        compiler_params=VMEM,
        name="filter_back",
    )(flags, grad, *pieces, taps)


def put_halves(target, sem, stage, parts):
    for i, part in enumerate(parts):
        high = part.astype(BF)
        stage[:, i] = high
        stage[:, len(parts) + i] = (part - high.astype(F32)).astype(BF)
    rows = target.shape[1]
    copy = pltpu.make_async_copy(
        stage, target.at[:, pl.ds(rows - TRAILER, TRAILER)], sem
    )
    copy.start()
    copy.wait()


def from_halves(received):
    halves = received[:, -TRAILER:].astype(F32)
    return halves[:, : TRAILER // 2] + halves[:, TRAILER // 2 :]


def coarse_body(block, query, key, grad, value, back, out, stage, sem, *, scale):
    del back
    q, k, g, v = query[...], key[...], grad[...], value[...]
    logits = mm(k, q, ((1,), (1,))) * scale
    expo = jnp.exp(logits - jnp.max(logits, axis=0, keepdims=True))
    w = expo / jnp.sum(expo, axis=0, keepdims=True)
    wr = w.astype(BF)
    slope = mm(v, g, ((1,), (1,)))
    delta = jnp.sum(wr.astype(F32) * slope, axis=0, keepdims=True)
    ds = (w * (slope - delta)).astype(BF)
    results = (
        mm(wr, v, ((0,), (0,))),
        mm(ds, k, ((0,), (0,))) * scale,
        mm(ds, q, ((1,), (0,))) * scale,
        mm(wr, g, ((1,), (0,))),
    )
    shape = (results[0].shape[0] // 8, 8, HEAD_DIM)
    mine = lax.broadcasted_iota(jnp.int32, shape, 1) == block[0]
    parts = [jnp.sum(jnp.where(mine, r.reshape(shape), 0.0), axis=1) for r in results]
    put_halves(out, sem, stage, parts)


def coarse_head(block, pooled, back, scale):
    anywhere = pl.BlockSpec(memory_space=pl.ANY)
    return pl.pallas_call(
        functools.partial(coarse_body, scale=scale),
        grid_spec=pltpu.PrefetchScalarGridSpec(
            num_scalar_prefetch=1,
            grid=(1,),
            in_specs=[whole(x.shape) for x in pooled] + [anywhere],
            out_specs=anywhere,
            scratch_shapes=[
                pltpu.VMEM((back.shape[0], TRAILER, HEAD_DIM), BF),
                pltpu.SemaphoreType.DMA,
            ],
        ),
        out_shape=jax.ShapeDtypeStruct(back.shape, back.dtype),
        input_output_aliases={5: 0},
        compiler_params=VMEM,
        name="coarse_head",
    )(block, *pooled, back)


def taps_body(member, grad, framed, out, wide):
    del member
    frames, height, breadth = grad.shape[:3]
    planes, rows = framed.shape[:2]
    for t in range(planes):
        for r in range(rows):
            wide[t * rows + r, 0 : framed.shape[2]] = framed[t, r].astype(F32)
    for col in range(3):
        sums = {}
        for t in range(planes):
            for r in range(rows):
                cells = wide[t * rows + r, col : col + breadth]
                for back in range(3):
                    for row in range(3):
                        f, y = t - 2 + back, r - row
                        if 0 <= f < frames and 0 <= y < height:
                            tap = 9 * back + 3 * row + col
                            term = jnp.sum((grad[f, y] * cells).reshape(-1, 8, 128), axis=0)
                            sums[tap] = sums[tap] + term if tap in sums else term
        for tap, total in sums.items():
            out[0, tap : tap + 1] = jnp.sum(total, axis=0, keepdims=True)
    out[0, 27:] = jnp.zeros((5, 128), F32)


def tap_gradients(member, grad, framed):
    return pl.pallas_call(
        taps_body,
        grid_spec=pltpu.PrefetchScalarGridSpec(
            num_scalar_prefetch=1,
            grid=(HEADS,),
            in_specs=[
                pl.BlockSpec(grad.shape[:3] + (128,), lambda i, m: (0, 0, 0, i)),
                pl.BlockSpec(framed.shape[:3] + (128,), lambda i, m: (0, 0, 0, i)),
            ],
            out_specs=pl.BlockSpec(
                (1, 32, 128), lambda i, m: ((i + HEADS - m[0]) % HEADS, 0, 0)
            ),
            scratch_shapes=[pltpu.VMEM((framed.shape[0] * framed.shape[1], 40, 128), F32)],
        ),
        out_shape=jax.ShapeDtypeStruct((HEADS, 32, 128), F32),
        compiler_params=VMEM,
        name="tap_gradients",
    )(member, grad, framed)


def shifted(block, steps):
    count = lax.axis_size("seq")
    return lax.ppermute(block, "seq", [(i, (i + steps) % count) for i in range(count)])


def with_neighbours(lattice, forward, place, ready, held):
    row_band, slab_index, col_half, band_count = place
    half = lax.axis_size("seq") // 2
    own = lattice.astype(BF)
    edge = jnp.where(col_half == 0, own[:, :, -1:], own[:, :, :1])
    frames = slice(-2, None) if forward else slice(0, 2)
    steps = band_count if forward else -band_count
    has_slab = slab_index > 0 if forward else slab_index < SLABS - 1
    own_edge = shifted(edge, half)
    near = shifted(own[frames], steps)
    near_edge = shifted(edge[frames], steps + half)
    near = jnp.where(has_slab, near, jnp.zeros_like(near)).astype(lattice.dtype)
    near_edge = jnp.where(has_slab, near_edge, jnp.zeros_like(near_edge))
    order = (lambda a, b: [a, b]) if forward else (lambda a, b: [b, a])
    middle = jnp.concatenate(order(near, lattice), axis=0)
    edges = jnp.concatenate(order(near_edge, own_edge), axis=0).astype(lattice.dtype)
    wide = side_columns(middle, edges, col_half)
    top, bottom = wide[:, :1].astype(BF), wide[:, -1:].astype(BF)
    top, bottom = together(top, bottom, ready)[:2]
    above, below, held = together(shifted(bottom, 1), shifted(top, -1), held)
    above = jnp.where(row_band > 0, above, jnp.zeros_like(above)).astype(lattice.dtype)
    below = jnp.where(row_band < band_count - 1, below, jnp.zeros_like(below))
    return jnp.concatenate([above, wide, below.astype(lattice.dtype)], axis=1), held


def to_lattice(tokens):
    channels = tokens.shape[1]
    cube_count = tokens.shape[0] // 64
    lattice = tokens.reshape(cube_count, 4, 4, 4, channels).transpose(1, 2, 0, 3, 4)
    return lattice.reshape(4, 4, cube_count * 4, channels)


def side_columns(lattice, edge, col_half):
    blank = jnp.zeros_like(edge)
    return jnp.concatenate(
        [jnp.where(col_half == 1, edge, blank), lattice, jnp.where(col_half == 0, edge, blank)],
        axis=2,
    )


def pool_cubes(tokens):
    return jnp.mean(
        tokens.astype(jnp.float32).reshape(tokens.shape[0] // 64, 64, tokens.shape[1]), axis=1
    )


def spread(per_cube):
    cube_count = per_cube.shape[0]
    return jnp.broadcast_to(per_cube[:, None, :], (cube_count, 64, per_cube.shape[1])).reshape(
        cube_count * 64, per_cube.shape[1]
    )


def exchanged(rows, groups=None):
    return lax.all_to_all(
        rows, "seq", split_axis=0, concat_axis=0, tiled=True, axis_index_groups=groups
    )


def in_plane(block, ahead):
    count = lax.axis_size("seq")
    return lax.ppermute(
        block, "seq", [(i, i // HEADS * HEADS + (i + ahead) % HEADS) for i in range(count)]
    )


def together(*values):
    return lax.optimization_barrier(values)


def shards(query_tokens, key_tokens, value_tokens, gate_tokens, filter_taps, selected, cotangent):
    devices = lax.axis_size("seq")
    device_index = lax.axis_index("seq")
    cube_count = query_tokens.shape[0] // 64
    pair_count = cube_count * HEADS
    channels = HEADS * HEAD_DIM
    capacity = max(3, 2 * HEADS * POOL // (devices - 1))
    logit_scale = HEAD_DIM ** (-0.5)
    band_count = devices // (2 * SLABS)
    rotated = (device_index + 2 * band_count + band_count // 2) % devices
    row_band = rotated % band_count
    slab_index = rotated // band_count % SLABS
    col_half = rotated // (devices // 2)

    owner_device = selected // cube_count
    pair_index = selected % cube_count * HEADS + jnp.arange(HEADS, dtype=jnp.int32)[None, :, None]
    owner_flat, pair_flat = owner_device.reshape(-1), pair_index.reshape(-1)
    remote_flat = owner_flat != device_index
    of_owner = (owner_flat[:, None] == jnp.arange(devices, dtype=jnp.int32)) & remote_flat[:, None]
    of_owner = of_owner.astype(BF)
    pair_ids = jnp.arange(pair_count, dtype=jnp.int32)
    of_pair = (pair_flat[:, None] == pair_ids).astype(BF)
    present = mm(of_owner, of_pair, ((0,), (0,))) > 0.5
    earlier = (pair_ids[:, None] < pair_ids).astype(BF)
    slot_rank = mm(present.astype(BF), earlier, ((1,), (0,)))
    in_slot = (slot_rank[:, None, :] == jnp.arange(capacity, dtype=F32)[None, :, None]) & (
        present[:, None, :]
    )
    requests = jnp.sum(jnp.where(in_slot, pair_ids, 0), axis=2).reshape(-1)
    asked_pairs = exchanged(requests)
    owner_rank = mm(of_owner, slot_rank.astype(BF), ((1,), (0,)))
    slot_of = jnp.sum(owner_rank * of_pair.astype(F32), axis=1).astype(jnp.int32)
    table_row = jnp.where(
        remote_flat, pair_count + owner_flat * capacity + slot_of, pair_flat
    )

    place = (row_band, slab_index, col_half, band_count)
    framed, asked_keys = with_neighbours(
        to_lattice(value_tokens), True, place, asked_pairs,
        gather_pairs(asked_pairs, key_tokens, devices),
    )
    far_keys = exchanged(asked_keys)

    filtered = filter_forward(framed, filter_taps)
    gated = cotangent.astype(F32) * gate_tokens.astype(F32)
    pooled = jnp.stack(
        [
            pool_cubes(query_tokens).astype(BF),
            pool_cubes(key_tokens).astype(BF),
            jnp.sum(gated.reshape(cube_count, 64, channels), axis=1).astype(BF),
            pool_cubes(filtered).astype(BF),
        ],
        axis=1,
    )
    pooled = pooled.reshape(cube_count, 4, HEADS, HEAD_DIM).transpose(2, 1, 0, 3)
    pooled = pooled.reshape(HEADS, 4 * cube_count, HEAD_DIM)
    far_values = exchanged(gather_pairs(asked_pairs, filtered, devices, pooled))
    one_head = far_values[:, capacity * 64 :].reshape(devices, 4, cube_count, HEAD_DIM)
    one_head = one_head.transpose(1, 0, 2, 3).reshape(4, devices * cube_count, HEAD_DIM)

    weights, own_value, back_value = fine_probs(
        table_row, query_tokens, cotangent, key_tokens, far_keys, capacity, logit_scale
    )
    block = (device_index // HEADS).reshape(1)
    back_value = exchanged(coarse_head(block, tuple(one_head), back_value, logit_scale))
    fine_out, fine_query, own_key, back_key = fine_grads(
        table_row, query_tokens, cotangent, key_tokens, far_keys, filtered, far_values, weights,
        capacity, logit_scale,
    )
    coarse = from_halves(back_value).reshape(cube_count, HEADS, 4, HEAD_DIM)
    coarse = coarse.transpose(2, 0, 1, 3).reshape(4, cube_count, channels)
    coarse_out, coarse_query = coarse[:2]

    coarse_tokens = spread(coarse_out)
    attended = (fine_out + gate_tokens.astype(F32) * coarse_tokens).astype(BF)
    gate_gradient = (cotangent.astype(F32) * coarse_tokens).astype(BF)
    query_gradient = (fine_query + spread(coarse_query) / 64.0).astype(BF)

    back_key, back_value = together(back_key, back_value)
    back_key = exchanged(back_key)
    grad_lattice, *pieces = collect(
        asked_pairs, own_value, back_value, back_value, col_half.reshape(1)
    )
    cells = [
        shifted(piece, rows - band_count * slabs + devices // 2 * halves)
        for piece, (_, (rows, slabs, halves)) in zip(pieces, PIECES)
    ]
    shares = tap_gradients((device_index % HEADS).reshape(1), grad_lattice, framed)
    mates = [in_plane(shares[ahead], ahead) for ahead in range(1, HEADS)]

    back_key, attended, query_gradient, gate_gradient, *arrived = together(
        back_key, attended, query_gradient, gate_gradient, *cells, *mates
    )
    cells, mates = arrived[: len(cells)], arrived[len(cells) :]
    taps = sum(mates, shares[0])
    rest = devices // HEADS
    columns = [[HEADS * b + h for b in range(rest)] for h in range(HEADS)]
    planes = [[HEADS * b + h for h in range(HEADS)] for b in range(rest)]
    taps = exchanged(jnp.broadcast_to(taps[None], (rest, 32, 128)), columns)
    (key_gradient,) = collect(asked_pairs, own_key, back_key, back_value)
    taps, key_gradient = together(taps, key_gradient)
    taps = jnp.sum(taps, axis=0)
    taps = exchanged(jnp.broadcast_to(taps[None], (HEADS, 32, 128)), planes)
    filter_gradient = taps.transpose(1, 0, 2).reshape(32, channels)[: filter_taps.shape[0]]
    flags = jnp.stack(
        [
            col_half,
            (slab_index < SLABS - 1).astype(jnp.int32),
            (row_band > 0).astype(jnp.int32),
            (row_band < band_count - 1).astype(jnp.int32),
        ]
    )
    value_gradient = filter_back(flags, grad_lattice, cells, filter_taps)
    return (attended, query_gradient, key_gradient, value_gradient, gate_gradient, filter_gradient)


def solution(mesh):
    return jax.shard_map(
        shards,
        mesh=mesh,
        in_specs=(
            P(("dp", "seq"), None),
            P(("dp", "seq"), None),
            P(("dp", "seq"), None),
            P(("dp", "seq"), None),
            P(),
            P(("dp", "seq"), None, None),
            P(("dp", "seq"), None),
        ),
        out_specs=(
            P(("dp", "seq"), None),
            P(("dp", "seq"), None),
            P(("dp", "seq"), None),
            P(("dp", "seq"), None),
            P(("dp", "seq"), None),
            P("dp", None),
        ),
        check_vma=False,
    )
```
